128 devices in a mesh: dp: 8 (over y_hi, x), tensor: 16 (over y_lo, z, core).
Axes of the slice: x: 4, y: 4 (y_hi: 2, y_lo: 2; y = y_hi * 2 + y_lo), z: 4, core: 2. Of those that a mesh axis runs over, the one named last changes fastest.
Arguments:
- images: bfloat16 [16384, 768], P('dp'), may hold values from -6 to 6
- head: bfloat16 [768, 768], P(None, 'tensor'), may hold values from -0.21875 to 0.21875
- tea_img: bfloat16 [16384, 1536], P('dp'), may hold values from -6 to 6
- stu_txt: bfloat16 [16384, 768], P(('dp', 'tensor')), may hold values from -6 to 6
- tea_txt: bfloat16 [16384, 1536], P(('dp', 'tensor')), may hold values from -6 to 6
Outputs:
- grad_images: float32 [16384, 768], P(('dp', 'tensor'))
- grad_head: float32 [768, 768], P(None, 'tensor')
- grad_text: float32 [16384, 768], P(('dp', 'tensor'))
The draws below stay inside these ranges and needn't reach their ends.
All inputs are finite; a program needn't handle non-finite values.
Results may differ from the reference program's by a relative error of at most 0.012.
Values may be sent and summed in bfloat16 or wider, within the bound.
A program may use at most 192 MiB of HBM per device.

```python
import math
import jax
import jax.numpy as jnp
from jax import lax

D_STU = 768
EMB = 768
D_TEA = 1536
PAIRS = 16384


def block_levels(key, shape, cuts, smallest, largest):
    factor_of, own = 1.0, jax.random.fold_in(key, 6)
    for dim, parts in cuts:
        heights = jnp.exp(jax.random.uniform(jax.random.fold_in(own, dim), (parts,), jnp.float32, smallest / len(cuts), largest / len(cuts)))
        factor_of = factor_of * jnp.repeat(heights, shape[dim] // parts).reshape([-1 if axis == dim else 1 for axis in range(len(shape))])
    return factor_of


def scatter_about(own_key, shape, scale, reach, cuts=(), kind=jnp.bfloat16):
    values = scale * jax.random.normal(own_key, shape, jnp.float32)
    if cuts:
        values = values * block_levels(own_key, shape, cuts, -0.22, 0.18)
    return jnp.clip(values, -reach, reach).astype(kind)


def setup_inputs(seed: int = 0) -> dict:
    splits = jax.random.split(jax.random.key(seed), 6)
    return {
        "images": scatter_about(splits[0], (PAIRS, D_STU), 1.0, 6.0, ((0, 8),)),
        "head": scatter_about(splits[1], (D_STU, EMB), D_STU ** -0.5, 0.21875, ((1, 16),)),
        "tea_img": scatter_about(splits[2], (PAIRS, D_TEA), 1.0, 6.0, ((0, 8),)),
        "stu_txt": scatter_about(splits[3], (PAIRS, EMB), 1.0, 6.0, ((0, 128),)),
        "tea_txt": scatter_about(splits[4], (PAIRS, D_TEA), 1.0, 6.0, ((0, 128),)),
    }


logit_scale = 64.0
logit_bias = -2.0
loss_scale = 65536.0

def normalize(values):
    floats = values.astype(jnp.float32)
    length = jnp.sqrt(lax.optimization_barrier(jnp.sum(floats * floats, axis=1, keepdims=True)) + 1e-06)
    return (floats / length, length)

def affinity_tile(img_emb, tea_img_emb, txt_piece, tea_piece, factor):
    contract = (((1,), (1,)), ((), ()))
    target = jax.nn.sigmoid(logit_scale * lax.dot_general(tea_img_emb, tea_piece, contract, preferred_element_type=jnp.float32) + logit_bias)
    student = logit_scale * lax.dot_general(img_emb, txt_piece, contract, preferred_element_type=jnp.float32) + logit_bias
    return ((jax.nn.sigmoid(student) - target) * factor).astype(jnp.bfloat16)

def reference(images, head, tea_img, stu_txt, tea_txt):
    pair_count = images.shape[0]
    emb_width = head.shape[1]
    factor = logit_scale * loss_scale / pair_count
    proj = jnp.dot(images, head, preferred_element_type=jnp.float32).astype(jnp.bfloat16)
    img_unit, proj_norm = normalize(proj)
    img_emb = img_unit.astype(jnp.bfloat16)
    tea_img_emb = normalize(tea_img)[0].astype(jnp.bfloat16)
    txt_unit, txt_norm = normalize(stu_txt)
    txt_emb = txt_unit.astype(jnp.bfloat16)
    tea_txt_emb = normalize(tea_txt)[0].astype(jnp.bfloat16)
    block = math.gcd(pair_count, 512)
    blocks = pair_count // block
    txt_blocks = txt_emb.reshape(blocks, block, emb_width)
    tea_blocks = tea_txt_emb.reshape(blocks, block, tea_txt.shape[1])

    def advance(img_grads, pieces):
        txt_piece, tea_piece = pieces
        coef = affinity_tile(img_emb, tea_img_emb, txt_piece, tea_piece, factor)
        img_grads = img_grads + jnp.dot(coef, txt_piece, preferred_element_type=jnp.float32)
        text_part = lax.dot_general(coef, img_emb, (((0,), (0,)), ((), ())), preferred_element_type=jnp.float32)
        return (img_grads, text_part)
    img_grads, text_parts = lax.scan(advance, jnp.zeros((pair_count, emb_width), jnp.float32), (txt_blocks, tea_blocks))
    txt_grads = text_parts.reshape(pair_count, emb_width)
    grad_proj = ((img_grads - img_unit * lax.optimization_barrier(jnp.sum(img_unit * img_grads, axis=1, keepdims=True))) / proj_norm).astype(jnp.bfloat16)
    grad_head = lax.dot_general(images, grad_proj, (((0,), (0,)), ((), ())), preferred_element_type=jnp.float32)
    grad_images = lax.dot_general(grad_proj, head, (((1,), (1,)), ((), ())), preferred_element_type=jnp.float32)
    grad_text = (txt_grads - txt_unit * lax.optimization_barrier(jnp.sum(txt_unit * txt_grads, axis=1, keepdims=True))) / txt_norm
    return (grad_images, grad_head, grad_text)
```

```python
import functools

import jax
import jax.numpy as jnp
from jax import lax
from jax.experimental import pallas as pl
from jax.experimental.pallas import tpu as pltpu
from jax.sharding import PartitionSpec as P

logit_scale = 64.0
logit_bias = -2.0
loss_scale = 65536.0

F32 = jnp.float32
BF16 = jnp.bfloat16
MESH = pl.DeviceIdType.MESH
NT = (((1,), (1,)), ((), ()))
NN = (((1,), (0,)), ((), ()))
EPS = 1e-06


def dot(a, b, dims=NN):
    return lax.dot_general(a, b, dims, preferred_element_type=F32)


def unit_of(values):
    floats = values.astype(F32)
    length = jnp.sqrt(jnp.sum(floats * floats, axis=1, keepdims=True) + EPS)
    inverse = 1.0 / length
    return floats * inverse, inverse


def kernel(
    factor,
    images_hbm,
    head_ref,
    tea_hbm,
    txt_hbm,
    teatxt_hbm,
    gi_ref,
    gh_ref,
    gt_ref,
    images,
    tea,
    rawtxt,
    rawtea,
    headg,
    img,
    img_t,
    tbuf,
    gimg,
    gacc,
    gown,
    gstage,
    grecv,
    pstage,
    precv,
    rstage,
    rrecv,
    rown,
    unit_own,
    inv_own,
    astage,
    arecv,
    xstage,
    xrecv,
    ystage,
    yrecv,
    lsem,
    hsend,
    hrecv,
    tsend,
    trecv,
    gsend,
    gsem,
    psend,
    psem,
    rsend,
    rsem,
    asend,
    asem,
    xsend,
    xsem,
    ysend,
    ysem,
):
    me_dp = lax.axis_index("dp")
    me_t = lax.axis_index("tensor")
    y_hi = me_dp // 4
    x = me_dp % 4
    chip = me_t // 2
    core = me_t % 2
    y_lo = me_t // 8
    flip_t = (1 - y_lo) * 8 + me_t % 8
    mate = chip * 2 + (1 - core)

    def at_x(dx):
        return y_hi * 4 + lax.rem(x + dx, 4)

    def across_x(dx):
        return (1 - y_hi) * 4 + lax.rem(x + dx, 4)

    def group(dx, side):
        if side == 0:
            return (at_x(dx), me_t)
        return (across_x(dx), flip_t)

    def plane(j):
        return (me_dp, lax.rem(chip + j, 8) * 2 + core)

    def remote(src, dst, ssem, rsem_, device):
        return pltpu.make_async_remote_copy(
            src_ref=src, dst_ref=dst, send_sem=ssem, recv_sem=rsem_, device_id=device, device_id_type=MESH
        )

    loads = [
        pltpu.make_async_copy(txt_hbm, rawtxt, lsem.at[0]),
        pltpu.make_async_copy(teatxt_hbm, rawtea, lsem.at[1]),
        pltpu.make_async_copy(tea_hbm, tea, lsem.at[2]),
        pltpu.make_async_copy(images_hbm, images, lsem.at[3]),
    ]
    for load in loads:
        load.start()

    partners = [group(dx, side) for dx in range(4) for side in range(2) if (dx, side) != (0, 0)]
    partners += [(me_dp, lax.rem(me_t + j, 16)) for j in range(1, 16)]
    partners += [((1 - y_hi) * 4 + x, me_t)]
    barrier = pltpu.get_barrier_semaphore()
    for device in partners:
        pl.semaphore_signal(barrier, inc=1, device_id=device, device_id_type=MESH)

    loads[0].wait()
    tbuf[0, 0, :, 0:768] = unit_of(rawtxt[...])[0].astype(BF16)
    loads[1].wait()
    tbuf[0, 0, :, 768:2304] = unit_of(rawtea[...])[0].astype(BF16)
    headg[chip, core] = head_ref[...]

    pl.semaphore_wait(barrier, len(partners))

    sends = []

    own = tbuf.at[0, 0]
    first = [
        remote(own, tbuf.at[0, 1], tsend.at[0], trecv.at[0], group(0, 1)),
        remote(own, tbuf.at[1, 1], tsend.at[1], trecv.at[2], group(1, 0)),
        remote(own, tbuf.at[1, 0], tsend.at[2], trecv.at[1], group(3, 0)),
    ]
    for copy in first:
        copy.start()
    sends += first

    heads = [
        remote(head_ref, headg.at[chip, core], hsend.at[j - 1], hrecv.at[chip], plane(j)) for j in range(1, 8)
    ]
    for copy in heads:
        copy.start()
    sends += heads

    loads[2].wait()

    @pl.loop(0, 32)
    def _(i):
        rows = pl.ds(pl.multiple_of(i * 64, 64), 64)
        tea[rows, :] = unit_of(tea[rows, :])[0].astype(BF16)

    for j in range(1, 8):
        other = lax.rem(chip + j, 8)
        remote(head_ref, headg.at[other, core], hsend.at[j - 1], hrecv.at[other], plane(j)).wait_recv()
    to_mate = remote(headg.at[:, core], headg.at[:, core], hsend.at[7], hrecv.at[8], (me_dp, mate))
    to_mate.start()
    sends.append(to_mate)
    loads[3].wait()
    remote(headg.at[:, 1 - core], headg.at[:, 1 - core], hsend.at[7], hrecv.at[8], (me_dp, mate)).wait_recv()

    def head_all():
        return headg[...].reshape(768, 768)

    @pl.loop(0, 8)
    def _(r):
        rows = pl.ds(pl.multiple_of(r * 256, 256), 256)
        proj = dot(images[rows, :], head_all(), NT).astype(BF16)
        unit = unit_of(proj)[0]
        img[rows, :] = unit.astype(BF16)
        img_t[r] = unit.T.astype(BF16)

    own_rows = pl.ds(pl.multiple_of(me_t * 128, 128), 128)
    unit, inverse = unit_of(dot(images[own_rows, :], head_all(), NT).astype(BF16))
    unit_own[...] = unit
    inv_own[...] = inverse

    def chunk(pair, r):
        rows = pl.ds(pl.multiple_of(r * 256, 256), 256)
        block = tbuf[pair].reshape(256, 2304)
        txt = block[:, 0:768]
        target = dot(tea[rows, :], block[:, 768:2304], NT)
        student = dot(img[rows, :], txt, NT)
        half = 0.5 * logit_scale
        coef = (
            (jnp.tanh(half * student + 0.5 * logit_bias) - jnp.tanh(half * target + 0.5 * logit_bias))
            * (0.5 * factor)
        ).astype(BF16)
        part = dot(coef, txt)
        if pair == 0:
            gimg[rows, :] = part
        else:
            gimg[rows, :] += part
        gacc[...] += dot(img_t[r], coef)

    def begin_step():
        gacc[...] = jnp.zeros_like(gacc)

    def wait_text(slot, pair, k, rows=None):
        ref = tbuf.at[pair, k] if rows is None else tbuf.at[pair, k, rows]
        remote(ref, ref, tsend.at[0], trecv.at[slot], group(0, 1)).wait_recv()

    def forward(src, dst, send, slot, device):
        copy = remote(src, dst, tsend.at[send], trecv.at[slot], device)
        copy.start()
        sends.append(copy)

    low, high = pl.ds(0, 64), pl.ds(64, 64)

    def send_text_grad(pair, k, device):
        index = pair * 2 + k
        mirror = {(0, 1): (0, 1), (1, 0): (1, 1), (1, 1): (1, 0), (2, 0): (2, 1), (2, 1): (2, 0), (3, 0): (3, 0), (3, 1): (3, 1)}
        there = mirror[(pair, k)]
        copy = remote(
            gstage.at[pair, k],
            grecv.at[there[0], there[1]],
            gsend.at[index],
            gsem.at[there[0] * 2 + there[1]],
            device,
        )
        copy.start()
        sends.append(copy)

    def stage_text_grads(pair):
        if pair == 0:
            gown[...] = gacc[:, 0:128]
        else:
            gstage[pair, 0] = gacc[:, 0:128].astype(BF16)
        gstage[pair, 1] = gacc[:, 128:256].astype(BF16)

    wait_text(0, 0, 1)
    forward(tbuf.at[0, 1], tbuf.at[2, 1], 3, 4, group(1, 0))
    forward(tbuf.at[0, 1], tbuf.at[2, 0], 4, 3, group(3, 0))
    wait_text(2, 1, 1)
    forward(tbuf.at[1, 1, low], tbuf.at[3, 0, low], 5, 5, group(1, 0))
    wait_text(1, 1, 0)
    forward(tbuf.at[1, 0, high], tbuf.at[3, 0, high], 6, 6, group(3, 0))
    begin_step()

    @pl.loop(0, 8)
    def _(r):
        chunk(0, r)

    stage_text_grads(0)
    send_text_grad(0, 1, group(0, 1))

    begin_step()

    @pl.loop(0, 8)
    def _(r):
        chunk(1, r)

    stage_text_grads(1)

    wait_text(4, 2, 1)
    forward(tbuf.at[2, 1, low], tbuf.at[3, 1, low], 7, 7, group(1, 0))
    wait_text(3, 2, 0)
    forward(tbuf.at[2, 0, high], tbuf.at[3, 1, high], 8, 8, group(3, 0))
    send_text_grad(1, 0, group(1, 0))
    send_text_grad(1, 1, group(3, 0))
    begin_step()

    @pl.loop(0, 8)
    def _(r):
        chunk(2, r)

    stage_text_grads(2)

    wait_text(5, 3, 0, low)
    wait_text(6, 3, 0, high)
    wait_text(7, 3, 1, low)
    wait_text(8, 3, 1, high)
    send_text_grad(2, 0, group(1, 1))
    send_text_grad(2, 1, group(3, 1))
    begin_step()

    def owner(k):
        return lax.rem(chip + 1 + k, 8)

    def from_mate(k):
        return remote(pstage.at[k], precv.at[k], psend.at[k], psem.at[k], (me_dp, mate))

    def to_owner(k):
        return remote(rstage.at[k], rrecv.at[chip], rsend.at[k], rsem.at[chip], (me_dp, owner(k) * 2 + core))

    def chip_sum(k):
        mine = pl.ds(pl.multiple_of(owner(k) * 256 + core * 128, 128), 128)
        from_mate(k).wait_recv()
        return gimg[mine, :] + precv[k].astype(F32)

    @pl.loop(0, 8)
    def _(k):
        r = owner(k)
        chunk(3, r)
        theirs = pl.ds(pl.multiple_of(r * 256 + (1 - core) * 128, 128), 128)
        pstage[k] = gimg[theirs, :].astype(BF16)
        from_mate(k).start()

        @pl.when(k > 0)
        def _():
            rstage[k - 1] = chip_sum(k - 1).astype(BF16)
            to_owner(k - 1).start()

    stage_text_grads(3)
    send_text_grad(3, 0, group(2, 0))
    send_text_grad(3, 1, group(2, 1))

    rown[...] = chip_sum(7)
    for j in range(1, 8):
        other = lax.rem(chip + j, 8)
        remote(rstage.at[0], rrecv.at[other], rsend.at[0], rsem.at[other], plane(j)).wait_recv()
        rown[...] += rrecv[other].astype(F32)

    total = rown[...]
    unit = unit_own[...]
    row_dot = jnp.sum(unit * total, axis=1, keepdims=True)
    grad_proj = (total - unit * row_dot) * inv_own[...]
    astage[...] = grad_proj.T.astype(BF16).reshape(16, 48, 128)
    arecv[me_t] = astage[me_t]
    scatter = []
    for j in range(1, 16):
        other = lax.rem(me_t + j, 16)
        copy = remote(astage.at[other], arecv.at[me_t], asend.at[j - 1], asem.at[me_t], (me_dp, other))
        copy.start()
        scatter.append(copy)
    sends += scatter

    gi_ref[...] = dot(grad_proj.astype(BF16), head_all())

    for j in range(1, 16):
        other = lax.rem(me_t + j, 16)
        remote(astage.at[other], arecv.at[other], asend.at[j - 1], asem.at[other], (me_dp, other)).wait_recv()

    head_part = jnp.zeros((48, 768), F32)
    for s in range(8):
        pieces = jnp.concatenate([arecv[2 * s], arecv[2 * s + 1]], axis=1)
        head_part += dot(pieces, images[s * 256 : (s + 1) * 256, :])
    xstage[...] = head_part.astype(BF16)
    xrecv[x] = xstage[...]
    for j in range(1, 4):
        copy = remote(xstage, xrecv.at[x], xsend.at[j - 1], xsem.at[x], (at_x(j), me_t))
        copy.start()
        sends.append(copy)

    text_sum = gown[...]
    for pair in range(4):
        for k in range(2):
            if (pair, k) != (0, 0):
                remote(
                    gstage.at[pair, k], grecv.at[pair, k], gsend.at[0], gsem.at[pair * 2 + k], group(0, 1)
                ).wait_recv()
                text_sum = text_sum + grecv[pair, k].astype(F32)
    text_grad = text_sum.T
    unit, inverse = unit_of(rawtxt[...])
    gt_ref[...] = (text_grad - unit * jnp.sum(unit * text_grad, axis=1, keepdims=True)) * inverse

    for j in range(1, 4):
        other = lax.rem(x + j, 4)
        remote(xstage, xrecv.at[other], xsend.at[j - 1], xsem.at[other], (at_x(j), me_t)).wait_recv()
    ystage[...] = (
        (xrecv[0].astype(F32) + xrecv[1].astype(F32)) + (xrecv[2].astype(F32) + xrecv[3].astype(F32))
    ).astype(BF16)
    swap = remote(ystage, yrecv, ysend.at[0], ysem.at[0], ((1 - y_hi) * 4 + x, me_t))
    swap.start()
    swap.wait_recv()
    sends.append(swap)
    gh_ref[...] = ystage[...].astype(F32) + yrecv[...].astype(F32)

    for copy in sends:
        copy.wait_send()

    @pl.loop(0, 8)
    def _(k):
        from_mate(k).wait_send()

        @pl.when(k < 7)
        def _():
            to_owner(k).wait_send()


def per_device(images, head, tea_img, stu_txt, tea_txt):
    factor = logit_scale * loss_scale / (images.shape[0] * lax.axis_size("dp"))
    any_spec = pl.BlockSpec(memory_space=pl.ANY)
    vmem_spec = pl.BlockSpec(memory_space=pltpu.VMEM)
    dma = pltpu.SemaphoreType.DMA
    grad_images, grad_head, grad_text = pl.pallas_call(
        functools.partial(kernel, factor),
        name="distill",
        out_shape=(
            jax.ShapeDtypeStruct((128, 768), F32),
            jax.ShapeDtypeStruct((48, 768), F32),
            jax.ShapeDtypeStruct((128, 768), F32),
        ),
        in_specs=[any_spec, vmem_spec, any_spec, any_spec, any_spec],
        out_specs=(vmem_spec, vmem_spec, vmem_spec),
        scratch_shapes=[
            pltpu.VMEM((2048, 768), BF16),
            pltpu.VMEM((2048, 1536), BF16),
            pltpu.VMEM((128, 768), BF16),
            pltpu.VMEM((128, 1536), BF16),
            pltpu.VMEM((8, 2, 48, 768), BF16),
            pltpu.VMEM((2048, 768), BF16),
            pltpu.VMEM((8, 768, 256), BF16),
            pltpu.VMEM((4, 2, 128, 2304), BF16),
            pltpu.VMEM((2048, 768), F32),
            pltpu.VMEM((768, 256), F32),
            pltpu.VMEM((768, 128), F32),
            pltpu.VMEM((4, 2, 768, 128), BF16),
            pltpu.VMEM((4, 2, 768, 128), BF16),
            pltpu.VMEM((8, 128, 768), BF16),
            pltpu.VMEM((8, 128, 768), BF16),
            pltpu.VMEM((8, 128, 768), BF16),
            pltpu.VMEM((8, 128, 768), BF16),
            pltpu.VMEM((128, 768), F32),
            pltpu.VMEM((128, 768), F32),
            pltpu.VMEM((128, 1), F32),
            pltpu.VMEM((16, 48, 128), BF16),
            pltpu.VMEM((16, 48, 128), BF16),
            pltpu.VMEM((48, 768), BF16),
            pltpu.VMEM((4, 48, 768), BF16),
            pltpu.VMEM((48, 768), BF16),
            pltpu.VMEM((48, 768), BF16),
            dma((4,)),
            dma((8,)),
            dma((9,)),
            dma((9,)),
            dma((9,)),
            dma((8,)),
            dma((8,)),
            dma((8,)),
            dma((8,)),
            dma((8,)),
            dma((8,)),
            dma((15,)),
            dma((16,)),
            dma((3,)),
            dma((4,)),
            dma((1,)),
            dma((1,)),
        ],
        compiler_params=pltpu.CompilerParams(
            collective_id=0, has_side_effects=True, vmem_limit_bytes=60 * 1024 * 1024
        ),
    )(images, head.T, tea_img, stu_txt, tea_txt)
    return (grad_images, grad_head.T, grad_text)


def solution(mesh):
    placed = (
        P("dp", None),
        P(None, "tensor"),
        P("dp", None),
        P(("dp", "tensor"), None),
        P(("dp", "tensor"), None),
    )
    return jax.shard_map(
        per_device,
        mesh=mesh,
        in_specs=placed,
        out_specs=(P(("dp", "tensor"), None), P(None, "tensor"), P(("dp", "tensor"), None)),
        check_vma=False,
    )
```

```python
import functools

import jax
import jax.numpy as jnp
from jax import lax
from jax.experimental import pallas as pl
from jax.experimental.pallas import tpu as pltpu
from jax.sharding import PartitionSpec as P

logit_scale = 64.0
logit_bias = -2.0
loss_scale = 65536.0

F32 = jnp.float32
BF16 = jnp.bfloat16
MESH = pl.DeviceIdType.MESH
NT = (((1,), (1,)), ((), ()))
NN = (((1,), (0,)), ((), ()))
EPS = 1e-06


def dot(a, b, dims=NN):
    return lax.dot_general(a, b, dims, preferred_element_type=F32)


def unit_of(values):
    floats = values.astype(F32)
    length = jnp.sqrt(jnp.sum(floats * floats, axis=1, keepdims=True) + EPS)
    inverse = 1.0 / length
    return floats * inverse, inverse


def kernel(
    factor,
    images_hbm,
    head_ref,
    tea_hbm,
    txt_hbm,
    teatxt_hbm,
    gi_ref,
    gh_ref,
    gt_ref,
    images,
    tea,
    rawtxt,
    rawtea,
    headg,
    img,
    img_t,
    tbuf,
    gimg,
    gacc,
    gown,
    gstage,
    grecv,
    pstage,
    precv,
    rstage,
    rrecv,
    rown,
    unit_own,
    inv_own,
    astage,
    arecv,
    xstage,
    xrecv,
    ystage,
    yrecv,
    lsem,
    hsend,
    hrecv,
    tsend,
    trecv,
    gsend,
    gsem,
    psend,
    psem,
    rsend,
    rsem,
    asend,
    asem,
    xsend,
    xsem,
    ysend,
    ysem,
):
    me_dp = lax.axis_index("dp")
    me_t = lax.axis_index("tensor")
    y_hi = me_dp // 4
    x = me_dp % 4
    chip = me_t // 2
    core = me_t % 2
    y_lo = me_t // 8
    flip_t = (1 - y_lo) * 8 + me_t % 8
    mate = chip * 2 + (1 - core)

    def at_x(dx):
        return y_hi * 4 + lax.rem(x + dx, 4)

    def across_x(dx):
        return (1 - y_hi) * 4 + lax.rem(x + dx, 4)

    def group(dx, side):
        if side == 0:
            return (at_x(dx), me_t)
        return (across_x(dx), flip_t)

    def plane(j):
        return (me_dp, lax.rem(chip + j, 8) * 2 + core)

    def remote(src, dst, ssem, rsem_, device):
        return pltpu.make_async_remote_copy(
            src_ref=src, dst_ref=dst, send_sem=ssem, recv_sem=rsem_, device_id=device, device_id_type=MESH
        )

    loads = [
        pltpu.make_async_copy(txt_hbm, rawtxt, lsem.at[0]),
        pltpu.make_async_copy(teatxt_hbm, rawtea, lsem.at[1]),
        pltpu.make_async_copy(tea_hbm, tea, lsem.at[2]),
        pltpu.make_async_copy(images_hbm, images, lsem.at[3]),
    ]
    for load in loads:
        load.start()

    partners = [group(dx, side) for dx in range(4) for side in range(2) if (dx, side) != (0, 0)]
    partners += [(me_dp, lax.rem(me_t + j, 16)) for j in range(1, 16)]
    partners += [((1 - y_hi) * 4 + x, me_t)]
    barrier = pltpu.get_barrier_semaphore()
    for device in partners:
        pl.semaphore_signal(barrier, inc=1, device_id=device, device_id_type=MESH)

    loads[0].wait()
    tbuf[0, 0:128, 0:768] = unit_of(rawtxt[...])[0].astype(BF16)
    loads[1].wait()
    tbuf[0, 0:128, 768:2304] = unit_of(rawtea[...])[0].astype(BF16)
    headg[chip, core] = head_ref[...]

    pl.semaphore_wait(barrier, len(partners))

    sends = []

    places = [
        (0, 128), (0, 192),
        (1, 0), (1, 64),
        (1, 128), (1, 192),
        (2, 0), (2, 64),
        (2, 128), (3, 64),
        (3, 0), (2, 192),
        (3, 128), (3, 192),
    ]

    def text_at(place):
        return tbuf.at[place[0], pl.ds(place[1], 64)]

    def send_text(src, index, send, device):
        copy = remote(text_at(src), text_at(places[index]), tsend.at[send], trecv.at[index], device)
        copy.start()
        sends.append(copy)

    def wait_text(*indices):
        for index in indices:
            ref = text_at(places[index])
            remote(ref, ref, tsend.at[0], trecv.at[index], across).wait_recv()

    across, ahead, behind = group(0, 1), group(1, 0), group(3, 0)
    own_low, own_high = (0, 0), (0, 64)
    send_text(own_low, 0, 0, across)
    send_text(own_low, 4, 1, ahead)
    send_text(own_high, 3, 2, behind)
    send_text(own_high, 1, 3, across)
    send_text(own_high, 5, 4, ahead)
    send_text(own_low, 2, 5, behind)

    heads = [
        remote(head_ref, headg.at[chip, core], hsend.at[j - 1], hrecv.at[chip], plane(j)) for j in range(1, 8)
    ]
    for copy in heads:
        copy.start()
    sends += heads

    loads[2].wait()

    @pl.loop(0, 32)
    def _(i):
        rows = pl.ds(pl.multiple_of(i * 64, 64), 64)
        tea[rows, :] = unit_of(tea[rows, :])[0].astype(BF16)

    for j in range(1, 8):
        other = lax.rem(chip + j, 8)
        remote(head_ref, headg.at[other, core], hsend.at[j - 1], hrecv.at[other], plane(j)).wait_recv()
    to_mate = remote(headg.at[:, core], headg.at[:, core], hsend.at[7], hrecv.at[8], (me_dp, mate))
    to_mate.start()
    sends.append(to_mate)
    loads[3].wait()
    remote(headg.at[:, 1 - core], headg.at[:, 1 - core], hsend.at[7], hrecv.at[8], (me_dp, mate)).wait_recv()

    def head_all():
        return headg[...].reshape(768, 768)

    def project(r):
        rows = pl.ds(pl.multiple_of(r * 256, 256), 256)
        proj = dot(images[rows, :], head_all(), NT).astype(BF16)
        unit = unit_of(proj)[0]
        img[rows, :] = unit.astype(BF16)
        img_t[r] = unit.T.astype(BF16)

    @pl.loop(0, 4)
    def _(r):
        project(r)

    wait_text(4, 3)
    send_text(places[4], 6, 6, ahead)
    send_text(places[3], 7, 7, behind)

    @pl.loop(4, 8)
    def _(r):
        project(r)

    own_rows = pl.ds(pl.multiple_of(me_t * 128, 128), 128)
    unit, inverse = unit_of(dot(images[own_rows, :], head_all(), NT).astype(BF16))
    unit_own[...] = unit
    inv_own[...] = inverse

    def coef_of(step, r):
        rows = pl.ds(pl.multiple_of(r * 256, 256), 256)
        target = dot(tea[rows, :], tbuf[step, :, 768:2304], NT)
        student = dot(img[rows, :], tbuf[step, :, 0:768], NT)
        half = 0.5 * logit_scale
        return (
            (jnp.tanh(half * student + 0.5 * logit_bias) - jnp.tanh(half * target + 0.5 * logit_bias))
            * (0.5 * factor)
        ).astype(BF16)

    def grads_of(step, r, coef, first):
        rows = pl.ds(pl.multiple_of(r * 256, 256), 256)
        part = dot(coef, tbuf[step, :, 0:768])
        if step == 0:
            gimg[rows, :] = part
        else:
            gimg[rows, :] += part
        text_part = dot(img_t[r], coef)
        if first:
            gacc[...] = text_part
        else:
            gacc[...] += text_part

    def run_step(step):
        coef = coef_of(step, 0)
        for r in range(8):
            later = coef_of(step, r + 1) if r < 7 else None
            grads_of(step, r, coef, r == 0)
            coef = later

    owners = [None, across, ahead, behind, group(2, 0), group(3, 1), group(1, 1), group(2, 1)]
    mirror = [0, 1, 3, 2, 4, 6, 5, 7]

    def send_text_grad(block):
        copy = remote(
            gstage.at[block],
            grecv.at[mirror[block]],
            gsend.at[block],
            gsem.at[mirror[block]],
            owners[block],
        )
        copy.start()
        sends.append(copy)

    wait_text(0, 1)
    send_text(places[0], 8, 8, ahead)
    send_text(places[1], 11, 9, behind)
    send_text(places[1], 9, 10, ahead)
    send_text(places[0], 10, 11, behind)
    run_step(0)
    gown[...] = gacc[:, 0:128]
    gstage[1] = gacc[:, 128:256].astype(BF16)
    send_text_grad(1)

    wait_text(2, 5)
    run_step(1)
    gstage[2] = gacc[:, 0:128].astype(BF16)
    gstage[3] = gacc[:, 128:256].astype(BF16)

    wait_text(6, 7)
    send_text(places[6], 12, 12, across)
    send_text(places[7], 13, 13, across)
    wait_text(8, 11)
    run_step(2)
    gstage[4] = gacc[:, 0:128].astype(BF16)
    gstage[5, :, 0:64] = gacc[:, 128:192].astype(BF16)
    gstage[6, :, 64:128] = gacc[:, 192:256].astype(BF16)

    wait_text(9, 10, 12, 13)
    for block in (2, 3, 4):
        send_text_grad(block)

    def owner(k):
        return lax.rem(chip + 1 + k, 8)

    def from_mate(k):
        return remote(pstage.at[k], precv.at[k], psend.at[k], psem.at[k], (me_dp, mate))

    def to_owner(k):
        return remote(rstage.at[k], rrecv.at[chip], rsend.at[k], rsem.at[chip], (me_dp, owner(k) * 2 + core))

    def to_mate_part(k):
        theirs = pl.ds(pl.multiple_of(owner(k) * 256 + (1 - core) * 128, 128), 128)
        pstage[k] = gimg[theirs, :].astype(BF16)
        from_mate(k).start()

    def chip_sum(k):
        mine = pl.ds(pl.multiple_of(owner(k) * 256 + core * 128, 128), 128)
        from_mate(k).wait_recv()
        return gimg[mine, :] + precv[k].astype(F32)

    def pass_on(k):
        rstage[k] = chip_sum(k).astype(BF16)
        to_owner(k).start()

    coef = coef_of(3, owner(0))
    for k in range(8):
        later = coef_of(3, owner(k + 1)) if k < 7 else None
        grads_of(3, owner(k), coef, k == 0)
        to_mate_part(k)
        if k > 0:
            pass_on(k - 1)
        coef = later

    gstage[6, :, 0:64] = gacc[:, 0:64].astype(BF16)
    gstage[5, :, 64:128] = gacc[:, 64:128].astype(BF16)
    gstage[7] = gacc[:, 128:256].astype(BF16)
    for block in (5, 6, 7):
        send_text_grad(block)

    rown[...] = chip_sum(7)
    for j in range(1, 8):
        other = lax.rem(chip + j, 8)
        remote(rstage.at[0], rrecv.at[other], rsend.at[0], rsem.at[other], plane(j)).wait_recv()
        rown[...] += rrecv[other].astype(F32)

    total = rown[...]
    unit = unit_own[...]
    row_dot = jnp.sum(unit * total, axis=1, keepdims=True)
    grad_proj = (total - unit * row_dot) * inv_own[...]
    astage[...] = grad_proj.T.astype(BF16).reshape(16, 48, 128)
    arecv[me_t] = astage[me_t]
    scatter = []
    for j in range(1, 16):
        other = lax.rem(me_t + j, 16)
        copy = remote(astage.at[other], arecv.at[me_t], asend.at[j - 1], asem.at[me_t], (me_dp, other))
        copy.start()
        scatter.append(copy)
    sends += scatter

    gi_ref[...] = dot(grad_proj.astype(BF16), head_all())

    for j in range(1, 16):
        other = lax.rem(me_t + j, 16)
        remote(astage.at[other], arecv.at[other], asend.at[j - 1], asem.at[other], (me_dp, other)).wait_recv()

    head_part = jnp.zeros((48, 768), F32)
    for s in range(8):
        pieces = jnp.concatenate([arecv[2 * s], arecv[2 * s + 1]], axis=1)
        head_part += dot(pieces, images[s * 256 : (s + 1) * 256, :])
    xstage[...] = head_part.astype(BF16)
    xrecv[x] = xstage[...]
    for j in range(1, 4):
        copy = remote(xstage, xrecv.at[x], xsend.at[j - 1], xsem.at[x], (at_x(j), me_t))
        copy.start()
        sends.append(copy)

    text_sum = gown[...]
    for block in range(1, 8):
        remote(gstage.at[block], grecv.at[block], gsend.at[block], gsem.at[block], across).wait_recv()
        text_sum = text_sum + grecv[block].astype(F32)
    text_grad = text_sum.T
    unit, inverse = unit_of(rawtxt[...])
    gt_ref[...] = (text_grad - unit * jnp.sum(unit * text_grad, axis=1, keepdims=True)) * inverse

    for j in range(1, 4):
        other = lax.rem(x + j, 4)
        remote(xstage, xrecv.at[other], xsend.at[j - 1], xsem.at[other], (at_x(j), me_t)).wait_recv()
    ystage[...] = (
        (xrecv[0].astype(F32) + xrecv[1].astype(F32)) + (xrecv[2].astype(F32) + xrecv[3].astype(F32))
    ).astype(BF16)
    swap = remote(ystage, yrecv, ysend.at[0], ysem.at[0], ((1 - y_hi) * 4 + x, me_t))
    swap.start()
    swap.wait_recv()
    sends.append(swap)
    gh_ref[...] = ystage[...].astype(F32) + yrecv[...].astype(F32)

    for copy in sends:
        copy.wait_send()

    @pl.loop(0, 8)
    def _(k):
        from_mate(k).wait_send()

        @pl.when(k < 7)
        def _():
            to_owner(k).wait_send()


def hand_over(*refs):
    half = len(refs) // 2
    for source, target in zip(refs[:half], refs[half:]):
        target[...] = source[...]


def per_device(images, head, tea_img, stu_txt, tea_txt):
    factor = logit_scale * loss_scale / (images.shape[0] * lax.axis_size("dp"))
    any_spec = pl.BlockSpec(memory_space=pl.ANY)
    vmem_spec = pl.BlockSpec(memory_space=pltpu.VMEM)
    dma = pltpu.SemaphoreType.DMA
    grad_images, grad_head, grad_text = pl.pallas_call(
        functools.partial(kernel, factor),
        name="distill",
        out_shape=(
            jax.ShapeDtypeStruct((128, 768), F32),
            jax.ShapeDtypeStruct((48, 768), F32),
            jax.ShapeDtypeStruct((128, 768), F32),
        ),
        in_specs=[any_spec, vmem_spec, any_spec, any_spec, any_spec],
        out_specs=(vmem_spec, vmem_spec, vmem_spec),
        scratch_shapes=[
            pltpu.VMEM((2048, 768), BF16),
            pltpu.VMEM((2048, 1536), BF16),
            pltpu.VMEM((128, 768), BF16),
            pltpu.VMEM((128, 1536), BF16),
            pltpu.VMEM((8, 2, 48, 768), BF16),
            pltpu.VMEM((2048, 768), BF16),
            pltpu.VMEM((8, 768, 256), BF16),
            pltpu.VMEM((4, 256, 2304), BF16),
            pltpu.VMEM((2048, 768), F32),
            pltpu.VMEM((768, 256), F32),
            pltpu.VMEM((768, 128), F32),
            pltpu.VMEM((8, 768, 128), BF16),
            pltpu.VMEM((8, 768, 128), BF16),
            pltpu.VMEM((8, 128, 768), BF16),
            pltpu.VMEM((8, 128, 768), BF16),
            pltpu.VMEM((8, 128, 768), BF16),
            pltpu.VMEM((8, 128, 768), BF16),
            pltpu.VMEM((128, 768), F32),
            pltpu.VMEM((128, 768), F32),
            pltpu.VMEM((128, 1), F32),
            pltpu.VMEM((16, 48, 128), BF16),
            pltpu.VMEM((16, 48, 128), BF16),
            pltpu.VMEM((48, 768), BF16),
            pltpu.VMEM((4, 48, 768), BF16),
            pltpu.VMEM((48, 768), BF16),
            pltpu.VMEM((48, 768), BF16),
            dma((4,)),
            dma((8,)),
            dma((9,)),
            dma((14,)),
            dma((14,)),
            dma((8,)),
            dma((8,)),
            dma((8,)),
            dma((8,)),
            dma((8,)),
            dma((8,)),
            dma((15,)),
            dma((16,)),
            dma((3,)),
            dma((4,)),
            dma((1,)),
            dma((1,)),
        ],
        compiler_params=pltpu.CompilerParams(
            collective_id=0, has_side_effects=True, vmem_limit_bytes=60 * 1024 * 1024
        ),
    )(images, head.T, tea_img, stu_txt, tea_txt)
    grad_images, grad_head, grad_text = pl.pallas_call(
        hand_over,
        name="hand_over",
        out_shape=tuple(jax.ShapeDtypeStruct(a.shape, a.dtype) for a in (grad_images, grad_head, grad_text)),
        in_specs=[vmem_spec] * 3,
        out_specs=(vmem_spec,) * 3,
    )(grad_images, grad_head, grad_text)
    return (grad_images, grad_head.T, grad_text)


def solution(mesh):
    placed = (
        P("dp", None),
        P(None, "tensor"),
        P("dp", None),
        P(("dp", "tensor"), None),
        P(("dp", "tensor"), None),
    )
    return jax.shard_map(
        per_device,
        mesh=mesh,
        in_specs=placed,
        out_specs=(P(("dp", "tensor"), None), P(None, "tensor"), P(("dp", "tensor"), None)),
        check_vma=False,
    )
```

```python
import functools

import jax
import jax.numpy as jnp
from jax import lax
from jax.experimental import pallas as pl
from jax.experimental.pallas import tpu as pltpu
from jax.sharding import PartitionSpec as P

logit_scale = 64.0
logit_bias = -2.0
loss_scale = 65536.0

F32 = jnp.float32
BF16 = jnp.bfloat16
MESH = pl.DeviceIdType.MESH
NT = (((1,), (1,)), ((), ()))
NN = (((1,), (0,)), ((), ()))
EPS = 1e-06


def dot(a, b, dims=NN):
    return lax.dot_general(a, b, dims, preferred_element_type=F32)


def unit_of(values):
    floats = values.astype(F32)
    length = jnp.sqrt(jnp.sum(floats * floats, axis=1, keepdims=True) + EPS)
    inverse = 1.0 / length
    return floats * inverse, inverse


def kernel(
    factor,
    images_hbm,
    head_ref,
    tea_hbm,
    txt_hbm,
    teatxt_hbm,
    gi_ref,
    gh_ref,
    gt_ref,
    images,
    tea,
    rawtxt,
    rawtea,
    headg,
    img,
    img_t,
    tbuf,
    gimg,
    gacc,
    gown,
    gstage,
    grecv,
    pstage,
    precv,
    rstage,
    rrecv,
    rown,
    units,
    invs,
    hacc,
    hpstage,
    hprecv,
    hrstage,
    hrrecv,
    xstage,
    xrecv,
    ystage,
    yrecv,
    lsem,
    hsend,
    hrecv,
    tsend,
    trecv,
    gsend,
    gsem,
    psend,
    psem,
    rsend,
    rsem,
    hpsend,
    hpsem,
    hrsend,
    hrsem,
    xsend,
    xsem,
    ysend,
    ysem,
):
    me_dp = lax.axis_index("dp")
    me_t = lax.axis_index("tensor")
    y_hi = me_dp // 4
    x = me_dp % 4
    chip = me_t // 2
    core = me_t % 2
    y_lo = me_t // 8
    flip_t = (1 - y_lo) * 8 + me_t % 8
    mate = chip * 2 + (1 - core)

    def at_x(dx):
        return y_hi * 4 + lax.rem(x + dx, 4)

    def across_x(dx):
        return (1 - y_hi) * 4 + lax.rem(x + dx, 4)

    def group(dx, side):
        if side == 0:
            return (at_x(dx), me_t)
        return (across_x(dx), flip_t)

    def plane(j):
        return (me_dp, lax.rem(chip + j, 8) * 2 + core)

    def remote(src, dst, ssem, rsem_, device):
        return pltpu.make_async_remote_copy(
            src_ref=src, dst_ref=dst, send_sem=ssem, recv_sem=rsem_, device_id=device, device_id_type=MESH
        )

    loads = [
        pltpu.make_async_copy(txt_hbm, rawtxt, lsem.at[0]),
        pltpu.make_async_copy(teatxt_hbm, rawtea, lsem.at[1]),
        pltpu.make_async_copy(tea_hbm, tea, lsem.at[2]),
        pltpu.make_async_copy(images_hbm, images, lsem.at[3]),
    ]
    for load in loads:
        load.start()

    partners = [group(dx, side) for dx in range(4) for side in range(2) if (dx, side) != (0, 0)]
    partners += [plane(j) for j in range(1, 8)] + [(me_dp, mate)]
    partners += [((1 - y_hi) * 4 + x, me_t)]
    barrier = pltpu.get_barrier_semaphore()
    for device in partners:
        pl.semaphore_signal(barrier, inc=1, device_id=device, device_id_type=MESH)

    loads[0].wait()
    tbuf[0, 0:128, 0:768] = unit_of(rawtxt[...])[0].astype(BF16)
    loads[1].wait()
    tbuf[0, 0:128, 768:2304] = unit_of(rawtea[...])[0].astype(BF16)
    headg[chip, core] = head_ref[...]

    pl.semaphore_wait(barrier, len(partners))

    sends = []

    places = [
        (0, 128), (0, 192),
        (1, 0), (1, 64),
        (1, 128), (1, 192),
        (2, 0), (2, 64),
        (2, 128), (3, 64),
        (3, 0), (2, 192),
        (3, 128), (3, 192),
    ]

    def text_at(place):
        return tbuf.at[place[0], pl.ds(place[1], 64)]

    def send_text(src, index, send, device):
        copy = remote(text_at(src), text_at(places[index]), tsend.at[send], trecv.at[index], device)
        copy.start()
        sends.append(copy)

    def wait_text(*indices):
        for index in indices:
            ref = text_at(places[index])
            remote(ref, ref, tsend.at[0], trecv.at[index], across).wait_recv()

    across, ahead, behind = group(0, 1), group(1, 0), group(3, 0)
    own_low, own_high = (0, 0), (0, 64)
    send_text(own_low, 0, 0, across)
    send_text(own_low, 4, 1, ahead)
    send_text(own_high, 3, 2, behind)
    send_text(own_high, 1, 3, across)
    send_text(own_high, 5, 4, ahead)
    send_text(own_low, 2, 5, behind)

    heads = [
        remote(head_ref, headg.at[chip, core], hsend.at[j - 1], hrecv.at[chip], plane(j)) for j in range(1, 8)
    ]
    for copy in heads:
        copy.start()
    sends += heads

    loads[2].wait()

    @pl.loop(0, 32)
    def _(i):
        rows = pl.ds(pl.multiple_of(i * 64, 64), 64)
        tea[rows, :] = unit_of(tea[rows, :])[0].astype(BF16)

    for j in range(1, 8):
        other = lax.rem(chip + j, 8)
        remote(head_ref, headg.at[other, core], hsend.at[j - 1], hrecv.at[other], plane(j)).wait_recv()
    to_mate = remote(headg.at[:, core], headg.at[:, core], hsend.at[7], hrecv.at[8], (me_dp, mate))
    to_mate.start()
    sends.append(to_mate)
    loads[3].wait()
    remote(headg.at[:, 1 - core], headg.at[:, 1 - core], hsend.at[7], hrecv.at[8], (me_dp, mate)).wait_recv()

    def head_all():
        return headg[...].reshape(768, 768)

    def project(r):
        rows = pl.ds(pl.multiple_of(r * 256, 256), 256)
        proj = dot(images[rows, :], head_all(), NT).astype(BF16)
        unit, inverse = unit_of(proj)
        units[rows, :] = unit
        invs[rows, :] = inverse
        img[rows, :] = unit.astype(BF16)
        img_t[r] = unit.T.astype(BF16)

    @pl.loop(0, 4)
    def _(r):
        project(r)

    wait_text(4, 3)
    send_text(places[4], 6, 6, ahead)
    send_text(places[3], 7, 7, behind)

    @pl.loop(4, 8)
    def _(r):
        project(r)

    def coef_of(step, r):
        rows = pl.ds(pl.multiple_of(r * 256, 256), 256)
        target = dot(tea[rows, :], tbuf[step, :, 768:2304], NT)
        student = dot(img[rows, :], tbuf[step, :, 0:768], NT)
        half = 0.5 * logit_scale
        return (
            (jnp.tanh(half * student + 0.5 * logit_bias) - jnp.tanh(half * target + 0.5 * logit_bias))
            * (0.5 * factor)
        ).astype(BF16)

    def grads_of(step, r, coef, first):
        rows = pl.ds(pl.multiple_of(r * 256, 256), 256)
        part = dot(coef, tbuf[step, :, 0:768])
        if step == 0:
            gimg[rows, :] = part
        else:
            gimg[rows, :] += part
        text_part = dot(img_t[r], coef)
        if first:
            gacc[...] = text_part
        else:
            gacc[...] += text_part

    def run_step(step):
        coef = coef_of(step, 0)
        for r in range(8):
            later = coef_of(step, r + 1) if r < 7 else None
            grads_of(step, r, coef, r == 0)
            coef = later

    owners = [None, across, ahead, behind, group(2, 0), group(3, 1), group(1, 1), group(2, 1)]
    mirror = [0, 1, 3, 2, 4, 6, 5, 7]

    def send_text_grad(block):
        copy = remote(
            gstage.at[block],
            grecv.at[mirror[block]],
            gsend.at[block],
            gsem.at[mirror[block]],
            owners[block],
        )
        copy.start()
        sends.append(copy)

    wait_text(0, 1)
    send_text(places[0], 8, 8, ahead)
    send_text(places[1], 11, 9, behind)
    send_text(places[1], 9, 10, ahead)
    send_text(places[0], 10, 11, behind)
    run_step(0)
    gown[...] = gacc[:, 0:128]
    gstage[1] = gacc[:, 128:256].astype(BF16)
    send_text_grad(1)

    wait_text(2, 5)
    run_step(1)
    gstage[2] = gacc[:, 0:128].astype(BF16)
    gstage[3] = gacc[:, 128:256].astype(BF16)

    wait_text(6, 7)
    send_text(places[6], 12, 12, across)
    send_text(places[7], 13, 13, across)
    wait_text(8, 11)
    run_step(2)
    gstage[4] = gacc[:, 0:128].astype(BF16)
    gstage[5, :, 0:64] = gacc[:, 128:192].astype(BF16)
    gstage[6, :, 64:128] = gacc[:, 192:256].astype(BF16)

    for block in (2, 3, 4):
        send_text_grad(block)
    wait_text(9, 10, 12, 13)

    def owner(k):
        return lax.rem(chip + 1 + k, 8)

    def from_mate(k):
        return remote(pstage.at[k], precv.at[k], psend.at[k], psem.at[k], (me_dp, mate))

    def to_owner(k):
        return remote(rstage.at[k], rrecv.at[chip], rsend.at[k], rsem.at[chip], (me_dp, owner(k) * 2 + core))

    def to_mate_part(k):
        theirs = pl.ds(pl.multiple_of(owner(k) * 256 + (1 - core) * 128, 128), 128)
        pstage[k] = gimg[theirs, :].astype(BF16)
        from_mate(k).start()

    def chip_sum(k):
        mine = pl.ds(pl.multiple_of(owner(k) * 256 + core * 128, 128), 128)
        from_mate(k).wait_recv()
        return gimg[mine, :] + precv[k].astype(F32)

    def pass_on(k):
        rstage[k] = chip_sum(k).astype(BF16)
        to_owner(k).start()

    def head_part(r, first):
        rows = pl.ds(pl.multiple_of(r * 256, 256), 256)
        grad, unit = gimg[rows, :], units[rows, :]
        row_dot = jnp.sum(unit * grad, axis=1, keepdims=True)
        grad_proj = (grad - unit * row_dot) * invs[rows, :]
        part = dot(grad_proj.T.astype(BF16), images[rows, :]).reshape(8, 2, 48, 768)
        if first:
            hacc[...] = part
        else:
            hacc[...] += part

    early = 3
    coef = coef_of(3, owner(0))
    for k in range(8):
        later = coef_of(3, owner(k + 1)) if k < 7 else None
        grads_of(3, owner(k), coef, k == 0)
        to_mate_part(k)
        head_part(owner(k), k == 0)
        if 0 < k <= early:
            pass_on(k - 1)
        coef = later

    hpstage[...] = hacc[:, 1 - core].astype(BF16)
    head_swap = remote(hpstage, hprecv, hpsend.at[0], hpsem.at[0], (me_dp, mate))
    head_swap.start()
    sends.append(head_swap)

    gstage[6, :, 0:64] = gacc[:, 0:64].astype(BF16)
    gstage[5, :, 64:128] = gacc[:, 64:128].astype(BF16)
    gstage[7] = gacc[:, 128:256].astype(BF16)
    for block in (5, 6, 7):
        send_text_grad(block)

    head_swap.wait_recv()
    hrstage[...] = (hacc[:, core] + hprecv[...].astype(F32)).astype(BF16)
    for j in range(1, 8):
        other = lax.rem(chip + j, 8)
        copy = remote(hrstage.at[other], hrrecv.at[chip], hrsend.at[j - 1], hrsem.at[chip], plane(j))
        copy.start()
        sends.append(copy)

    for k in range(early, 7):
        pass_on(k)
    rown[...] = chip_sum(7)

    head_sum = hrstage[chip].astype(F32)
    for j in range(1, 8):
        other = lax.rem(chip + j, 8)
        remote(hrstage.at[0], hrrecv.at[other], hrsend.at[0], hrsem.at[other], plane(j)).wait_recv()
        head_sum = head_sum + hrrecv[other].astype(F32)
    xstage[...] = head_sum.astype(BF16)
    xrecv[x] = xstage[...]
    for j in range(1, 4):
        copy = remote(xstage, xrecv.at[x], xsend.at[j - 1], xsem.at[x], (at_x(j), me_t))
        copy.start()
        sends.append(copy)

    text_sum = gown[...]
    for block in range(1, 8):
        remote(gstage.at[block], grecv.at[block], gsend.at[block], gsem.at[block], across).wait_recv()
        text_sum = text_sum + grecv[block].astype(F32)
    text_grad = text_sum.T
    unit, inverse = unit_of(rawtxt[...])
    gt_ref[...] = (text_grad - unit * jnp.sum(unit * text_grad, axis=1, keepdims=True)) * inverse

    for j in range(1, 4):
        other = lax.rem(x + j, 4)
        remote(xstage, xrecv.at[other], xsend.at[j - 1], xsem.at[other], (at_x(j), me_t)).wait_recv()
    ystage[...] = (
        (xrecv[0].astype(F32) + xrecv[1].astype(F32)) + (xrecv[2].astype(F32) + xrecv[3].astype(F32))
    ).astype(BF16)
    swap = remote(ystage, yrecv, ysend.at[0], ysem.at[0], ((1 - y_hi) * 4 + x, me_t))
    swap.start()
    sends.append(swap)

    for j in range(1, 8):
        other = lax.rem(chip + j, 8)
        remote(rstage.at[0], rrecv.at[other], rsend.at[0], rsem.at[other], plane(j)).wait_recv()
        rown[...] += rrecv[other].astype(F32)
    own_rows = pl.ds(pl.multiple_of(me_t * 128, 128), 128)
    total, unit = rown[...], units[own_rows, :]
    row_dot = jnp.sum(unit * total, axis=1, keepdims=True)
    grad_proj = (total - unit * row_dot) * invs[own_rows, :]
    gi_ref[...] = dot(grad_proj.astype(BF16), head_all())

    swap.wait_recv()
    gh_ref[...] = ystage[...].astype(F32) + yrecv[...].astype(F32)

    for copy in sends:
        copy.wait_send()

    @pl.loop(0, 8)
    def _(k):
        from_mate(k).wait_send()

        @pl.when(k < 7)
        def _():
            to_owner(k).wait_send()


def hand_over(*refs):
    half = len(refs) // 2
    for source, target in zip(refs[:half], refs[half:]):
        target[...] = source[...]


def per_device(images, head, tea_img, stu_txt, tea_txt):
    factor = logit_scale * loss_scale / (images.shape[0] * lax.axis_size("dp"))
    any_spec = pl.BlockSpec(memory_space=pl.ANY)
    vmem_spec = pl.BlockSpec(memory_space=pltpu.VMEM)
    dma = pltpu.SemaphoreType.DMA
    grad_images, grad_head, grad_text = pl.pallas_call(
        functools.partial(kernel, factor),
        name="distill",
        out_shape=(
            jax.ShapeDtypeStruct((128, 768), F32),
            jax.ShapeDtypeStruct((48, 768), F32),
            jax.ShapeDtypeStruct((128, 768), F32),
        ),
        in_specs=[any_spec, vmem_spec, any_spec, any_spec, any_spec],
        out_specs=(vmem_spec, vmem_spec, vmem_spec),
        scratch_shapes=[
            pltpu.VMEM((2048, 768), BF16),
            pltpu.VMEM((2048, 1536), BF16),
            pltpu.VMEM((128, 768), BF16),
            pltpu.VMEM((128, 1536), BF16),
            pltpu.VMEM((8, 2, 48, 768), BF16),
            pltpu.VMEM((2048, 768), BF16),
            pltpu.VMEM((8, 768, 256), BF16),
            pltpu.VMEM((4, 256, 2304), BF16),
            pltpu.VMEM((2048, 768), F32),
            pltpu.VMEM((768, 256), F32),
            pltpu.VMEM((768, 128), F32),
            pltpu.VMEM((8, 768, 128), BF16),
            pltpu.VMEM((8, 768, 128), BF16),
            pltpu.VMEM((8, 128, 768), BF16),
            pltpu.VMEM((8, 128, 768), BF16),
            pltpu.VMEM((8, 128, 768), BF16),
            pltpu.VMEM((8, 128, 768), BF16),
            pltpu.VMEM((128, 768), F32),
            pltpu.VMEM((2048, 768), F32),
            pltpu.VMEM((2048, 1), F32),
            pltpu.VMEM((8, 2, 48, 768), F32),
            pltpu.VMEM((8, 48, 768), BF16),
            pltpu.VMEM((8, 48, 768), BF16),
            pltpu.VMEM((8, 48, 768), BF16),
            pltpu.VMEM((8, 48, 768), BF16),
            pltpu.VMEM((48, 768), BF16),
            pltpu.VMEM((4, 48, 768), BF16),
            pltpu.VMEM((48, 768), BF16),
            pltpu.VMEM((48, 768), BF16),
            dma((4,)),
            dma((8,)),
            dma((9,)),
            dma((14,)),
            dma((14,)),
            dma((8,)),
            dma((8,)),
            dma((8,)),
            dma((8,)),
            dma((8,)),
            dma((8,)),
            dma((1,)),
            dma((1,)),
            dma((7,)),
            dma((8,)),
            dma((3,)),
            dma((4,)),
            dma((1,)),
            dma((1,)),
        ],
        compiler_params=pltpu.CompilerParams(
            collective_id=0, has_side_effects=True, vmem_limit_bytes=60 * 1024 * 1024
        ),
    )(images, head.T, tea_img, stu_txt, tea_txt)
    grad_images, grad_head, grad_text = pl.pallas_call(
        hand_over,
        name="hand_over",
        out_shape=tuple(jax.ShapeDtypeStruct(a.shape, a.dtype) for a in (grad_images, grad_head, grad_text)),
        in_specs=[vmem_spec] * 3,
        out_specs=(vmem_spec,) * 3,
    )(grad_images, grad_head, grad_text)
    return (grad_images, grad_head.T, grad_text)


def solution(mesh):
    placed = (
        P("dp", None),
        P(None, "tensor"),
        P("dp", None),
        P(("dp", "tensor"), None),
        P(("dp", "tensor"), None),
    )
    return jax.shard_map(
        per_device,
        mesh=mesh,
        in_specs=placed,
        out_specs=(P(("dp", "tensor"), None), P(None, "tensor"), P(("dp", "tensor"), None)),
        check_vma=False,
    )
```

```python
import functools

import jax
import jax.numpy as jnp
from jax import lax
from jax.experimental import pallas as pl
from jax.experimental.pallas import tpu as pltpu
from jax.sharding import PartitionSpec as P

logit_scale = 64.0
logit_bias = -2.0
loss_scale = 65536.0

F32 = jnp.float32
BF16 = jnp.bfloat16
MESH = pl.DeviceIdType.MESH
NT = (((1,), (1,)), ((), ()))
NN = (((1,), (0,)), ((), ()))
EPS = 1e-06


def dot(a, b, dims=NN):
    return lax.dot_general(a, b, dims, preferred_element_type=F32)


def unit_of(values):
    floats = values.astype(F32)
    length = jnp.sqrt(jnp.sum(floats * floats, axis=1, keepdims=True) + EPS)
    inverse = 1.0 / length
    return floats * inverse, inverse


def kernel(
    factor,
    images_hbm,
    head_ref,
    tea_hbm,
    txt_hbm,
    teatxt_hbm,
    gi_ref,
    gh_ref,
    gt_ref,
    images,
    tea,
    rawtxt,
    rawtea,
    headg,
    img,
    img_t,
    tbuf,
    gimg,
    gacc,
    gown,
    gstage,
    grecv,
    pstage,
    precv,
    rstage,
    rrecv,
    rown,
    units,
    invs,
    hacc,
    hpstage,
    hprecv,
    hrstage,
    hrrecv,
    xstage,
    xrecv,
    lsem,
    hsend,
    hrecv,
    tsend,
    trecv,
    gsend,
    gsem,
    psend,
    psem,
    rsend,
    rsem,
    hpsend,
    hpsem,
    hrsend,
    hrsem,
    xsend,
    xsem,
):
    me_dp = lax.axis_index("dp")
    me_t = lax.axis_index("tensor")
    y_hi = me_dp // 4
    x = me_dp % 4
    chip = me_t // 2
    core = me_t % 2
    y_lo = me_t // 8
    flip_t = (1 - y_lo) * 8 + me_t % 8
    mate = chip * 2 + (1 - core)

    def at_x(dx):
        return y_hi * 4 + lax.rem(x + dx, 4)

    def across_x(dx):
        return (1 - y_hi) * 4 + lax.rem(x + dx, 4)

    def group(dx, side):
        if side == 0:
            return (at_x(dx), me_t)
        return (across_x(dx), flip_t)

    def plane(j):
        return (me_dp, lax.rem(chip + j, 8) * 2 + core)

    def remote(src, dst, ssem, rsem_, device):
        return pltpu.make_async_remote_copy(
            src_ref=src, dst_ref=dst, send_sem=ssem, recv_sem=rsem_, device_id=device, device_id_type=MESH
        )

    loads = [
        pltpu.make_async_copy(txt_hbm, rawtxt, lsem.at[0]),
        pltpu.make_async_copy(teatxt_hbm, rawtea, lsem.at[1]),
        pltpu.make_async_copy(tea_hbm, tea, lsem.at[2]),
        pltpu.make_async_copy(images_hbm, images, lsem.at[3]),
    ]
    for load in loads:
        load.start()

    partners = [group(dx, side) for dx in range(4) for side in range(2) if (dx, side) != (0, 0)]
    partners += [plane(j) for j in range(1, 8)] + [(me_dp, mate)]
    partners += [(across_x(dx), me_t) for dx in range(4)]
    barrier = pltpu.get_barrier_semaphore()
    for device in partners:
        pl.semaphore_signal(barrier, inc=1, device_id=device, device_id_type=MESH)

    loads[0].wait()
    tbuf[0, 0:128, 0:768] = unit_of(rawtxt[...])[0].astype(BF16)
    loads[1].wait()
    tbuf[0, 0:128, 768:2304] = unit_of(rawtea[...])[0].astype(BF16)
    headg[chip, core] = head_ref[...]

    pl.semaphore_wait(barrier, len(partners))

    sends = []

    places = [
        (0, 128), (0, 192),
        (1, 0), (1, 64),
        (1, 128), (1, 192),
        (2, 0), (2, 64),
        (2, 128), (3, 64),
        (2, 192), (3, 0),
        (3, 128), (3, 192),
    ]

    def text_at(place):
        return tbuf.at[place[0], pl.ds(place[1], 64)]

    def send_text(src, index, send, device):
        copy = remote(text_at(src), text_at(places[index]), tsend.at[send], trecv.at[index], device)
        copy.start()
        sends.append(copy)

    def wait_text(*indices):
        for index in indices:
            ref = text_at(places[index])
            remote(ref, ref, tsend.at[0], trecv.at[index], across).wait_recv()

    across, ahead, behind = group(0, 1), group(1, 0), group(3, 0)
    own_low, own_high = (0, 0), (0, 64)
    send_text(own_low, 0, 0, across)
    send_text(own_low, 4, 1, ahead)
    send_text(own_high, 3, 2, behind)
    send_text(own_high, 1, 3, across)
    send_text(own_high, 5, 4, ahead)
    send_text(own_low, 2, 5, behind)

    heads = [
        remote(head_ref, headg.at[chip, core], hsend.at[j - 1], hrecv.at[chip], plane(j)) for j in range(1, 8)
    ]
    for copy in heads:
        copy.start()
    sends += heads

    loads[2].wait()

    @pl.loop(0, 32)
    def _(i):
        rows = pl.ds(pl.multiple_of(i * 64, 64), 64)
        tea[rows, :] = unit_of(tea[rows, :])[0].astype(BF16)

    for j in range(1, 8):
        other = lax.rem(chip + j, 8)
        remote(head_ref, headg.at[other, core], hsend.at[j - 1], hrecv.at[other], plane(j)).wait_recv()
    to_mate = remote(headg.at[:, core], headg.at[:, core], hsend.at[7], hrecv.at[8], (me_dp, mate))
    to_mate.start()
    sends.append(to_mate)
    loads[3].wait()
    remote(headg.at[:, 1 - core], headg.at[:, 1 - core], hsend.at[7], hrecv.at[8], (me_dp, mate)).wait_recv()

    def head_all():
        return headg[...].reshape(768, 768)

    def project(r):
        rows = pl.ds(pl.multiple_of(r * 256, 256), 256)
        proj = dot(images[rows, :], head_all(), NT).astype(BF16)
        unit, inverse = unit_of(proj)
        units[rows, :] = unit
        invs[rows, :] = inverse
        img[rows, :] = unit.astype(BF16)
        img_t[r] = unit.T.astype(BF16)

    @pl.loop(0, 4)
    def _(r):
        project(r)

    wait_text(4, 3)
    send_text(places[4], 6, 6, ahead)
    send_text(places[3], 7, 7, behind)
    wait_text(0)
    send_text(places[0], 8, 8, ahead)
    send_text(places[0], 10, 11, behind)

    @pl.loop(4, 8)
    def _(r):
        project(r)

    def coef_of(step, r):
        rows = pl.ds(pl.multiple_of(r * 256, 256), 256)
        target = dot(tea[rows, :], tbuf[step, :, 768:2304], NT)
        student = dot(img[rows, :], tbuf[step, :, 0:768], NT)
        half = 0.5 * logit_scale
        return (
            (jnp.tanh(half * student + 0.5 * logit_bias) - jnp.tanh(half * target + 0.5 * logit_bias))
            * (0.5 * factor)
        ).astype(BF16)

    def grads_of(step, r, coef, first):
        rows = pl.ds(pl.multiple_of(r * 256, 256), 256)
        part = dot(coef, tbuf[step, :, 0:768])
        if step == 0:
            gimg[rows, :] = part
        else:
            gimg[rows, :] += part
        text_part = dot(img_t[r], coef)
        if first:
            gacc[...] = text_part
        else:
            gacc[...] += text_part

    def run_step(step, pause=None, meanwhile=None):
        coef = coef_of(step, 0)
        for r in range(8):
            if r == pause:
                meanwhile()
            later = coef_of(step, r + 1) if r < 7 else None
            grads_of(step, r, coef, r == 0)
            coef = later

    owners = [None, across, ahead, behind, group(2, 0), group(3, 1), group(1, 1), group(2, 1)]
    mirror = [0, 1, 3, 2, 4, 6, 5, 7]

    def send_text_grad(block):
        copy = remote(
            gstage.at[block],
            grecv.at[mirror[block]],
            gsend.at[block],
            gsem.at[mirror[block]],
            owners[block],
        )
        copy.start()
        sends.append(copy)

    wait_text(1)
    send_text(places[1], 9, 10, ahead)
    send_text(places[1], 11, 9, behind)
    run_step(0)
    gown[...] = gacc[:, 0:128]
    gstage[1] = gacc[:, 128:256].astype(BF16)
    send_text_grad(1)

    wait_text(2, 5)

    def second_across():
        wait_text(6, 7)
        send_text(places[6], 12, 12, across)
        send_text(places[7], 13, 13, across)

    run_step(1, 5, second_across)
    gstage[2] = gacc[:, 0:128].astype(BF16)
    gstage[3] = gacc[:, 128:256].astype(BF16)

    wait_text(8, 10)
    run_step(2)
    gstage[4] = gacc[:, 0:128].astype(BF16)
    gstage[5, :, 0:64] = gacc[:, 128:192].astype(BF16)
    gstage[6, :, 0:64] = gacc[:, 192:256].astype(BF16)

    for block in (2, 3, 4):
        send_text_grad(block)
    wait_text(9, 11, 12, 13)

    def owner(k):
        return lax.rem(chip + 1 + k, 8)

    def from_mate(k):
        return remote(pstage.at[k], precv.at[k], psend.at[k], psem.at[k], (me_dp, mate))

    def to_owner(k):
        return remote(rstage.at[k], rrecv.at[chip], rsend.at[k], rsem.at[chip], (me_dp, owner(k) * 2 + core))

    def to_mate_part(k):
        theirs = pl.ds(pl.multiple_of(owner(k) * 256 + (1 - core) * 128, 128), 128)
        pstage[k] = gimg[theirs, :].astype(BF16)
        from_mate(k).start()

    def chip_sum(k):
        mine = pl.ds(pl.multiple_of(owner(k) * 256 + core * 128, 128), 128)
        from_mate(k).wait_recv()
        return gimg[mine, :] + precv[k].astype(F32)

    def pass_on(k):
        rstage[k] = chip_sum(k).astype(BF16)
        to_owner(k).start()

    def head_part(r, first):
        rows = pl.ds(pl.multiple_of(r * 256, 256), 256)
        grad, unit = gimg[rows, :], units[rows, :]
        row_dot = jnp.sum(unit * grad, axis=1, keepdims=True)
        grad_proj = (grad - unit * row_dot) * invs[rows, :]
        part = dot(grad_proj.T.astype(BF16), images[rows, :]).reshape(8, 2, 48, 768)
        if first:
            hacc[...] = part
        else:
            hacc[...] += part

    lag, early = 4, 4
    coef = coef_of(3, owner(0))
    for k in range(8):
        later = coef_of(3, owner(k + 1)) if k < 7 else None
        grads_of(3, owner(k), coef, k == 0)
        to_mate_part(k)
        head_part(owner(k), k == 0)
        if k >= lag:
            pass_on(k - lag)
        coef = later

    hpstage[...] = hacc[:, 1 - core].astype(BF16)
    head_swap = remote(hpstage, hprecv, hpsend.at[0], hpsem.at[0], (me_dp, mate))
    head_swap.start()
    sends.append(head_swap)

    gstage[6, :, 64:128] = gacc[:, 0:64].astype(BF16)
    gstage[5, :, 64:128] = gacc[:, 64:128].astype(BF16)
    gstage[7] = gacc[:, 128:256].astype(BF16)
    for block in (5, 6, 7):
        send_text_grad(block)

    head_swap.wait_recv()
    hrstage[...] = (hacc[:, core] + hprecv[...].astype(F32)).astype(BF16)
    for j in range(1, 8):
        other = lax.rem(chip + j, 8)
        copy = remote(hrstage.at[other], hrrecv.at[chip], hrsend.at[j - 1], hrsem.at[chip], plane(j))
        copy.start()
        sends.append(copy)

    for k in range(early, 7):
        pass_on(k)
    rown[...] = chip_sum(7)

    head_sum = hrstage[chip].astype(F32)
    for j in range(1, 8):
        other = lax.rem(chip + j, 8)
        remote(hrstage.at[0], hrrecv.at[other], hrsend.at[0], hrsem.at[other], plane(j)).wait_recv()
        head_sum = head_sum + hrrecv[other].astype(F32)
    xstage[...] = head_sum.astype(BF16)
    xrecv[me_dp] = xstage[...]
    others = [at_x(1), at_x(3), across_x(0), at_x(2), across_x(1), across_x(3), across_x(2)]
    for j, other in enumerate(others):
        copy = remote(xstage, xrecv.at[me_dp], xsend.at[j], xsem.at[me_dp], (other, me_t))
        copy.start()
        sends.append(copy)

    text_sum = gown[...]
    for block in range(1, 8):
        remote(gstage.at[block], grecv.at[block], gsend.at[block], gsem.at[block], across).wait_recv()
        text_sum = text_sum + grecv[block].astype(F32)
    text_grad = text_sum.T
    unit, inverse = unit_of(rawtxt[...])
    gt_ref[...] = (text_grad - unit * jnp.sum(unit * text_grad, axis=1, keepdims=True)) * inverse

    for j in range(1, 8):
        other = lax.rem(chip + j, 8)
        remote(rstage.at[0], rrecv.at[other], rsend.at[0], rsem.at[other], plane(j)).wait_recv()
        rown[...] += rrecv[other].astype(F32)
    own_rows = pl.ds(pl.multiple_of(me_t * 128, 128), 128)
    total, unit = rown[...], units[own_rows, :]
    row_dot = jnp.sum(unit * total, axis=1, keepdims=True)
    grad_proj = (total - unit * row_dot) * invs[own_rows, :]
    gi_ref[...] = dot(grad_proj.astype(BF16), head_all())

    for other in others:
        remote(xstage, xrecv.at[other], xsend.at[0], xsem.at[other], (other, me_t)).wait_recv()
    head_grad = xrecv[0].astype(F32)
    for d in range(1, 8):
        head_grad = head_grad + xrecv[d].astype(F32)
    gh_ref[...] = head_grad

    for copy in sends:
        copy.wait_send()

    @pl.loop(0, 8)
    def _(k):
        from_mate(k).wait_send()

        @pl.when(k < 7)
        def _():
            to_owner(k).wait_send()


def hand_over(*refs):
    half = len(refs) // 2
    for source, target in zip(refs[:half], refs[half:]):
        target[...] = source[...]


def per_device(images, head, tea_img, stu_txt, tea_txt):
    factor = logit_scale * loss_scale / (images.shape[0] * lax.axis_size("dp"))
    any_spec = pl.BlockSpec(memory_space=pl.ANY)
    vmem_spec = pl.BlockSpec(memory_space=pltpu.VMEM)
    dma = pltpu.SemaphoreType.DMA
    grad_images, grad_head, grad_text = pl.pallas_call(
        functools.partial(kernel, factor),
        name="distill",
        out_shape=(
            jax.ShapeDtypeStruct((128, 768), F32),
            jax.ShapeDtypeStruct((48, 768), F32),
            jax.ShapeDtypeStruct((128, 768), F32),
        ),
        in_specs=[any_spec, vmem_spec, any_spec, any_spec, any_spec],
        out_specs=(vmem_spec, vmem_spec, vmem_spec),
        scratch_shapes=[
            pltpu.VMEM((2048, 768), BF16),
            pltpu.VMEM((2048, 1536), BF16),
            pltpu.VMEM((128, 768), BF16),
            pltpu.VMEM((128, 1536), BF16),
            pltpu.VMEM((8, 2, 48, 768), BF16),
            pltpu.VMEM((2048, 768), BF16),
            pltpu.VMEM((8, 768, 256), BF16),
            pltpu.VMEM((4, 256, 2304), BF16),
            pltpu.VMEM((2048, 768), F32),
            pltpu.VMEM((768, 256), F32),
            pltpu.VMEM((768, 128), F32),
            pltpu.VMEM((8, 768, 128), BF16),
            pltpu.VMEM((8, 768, 128), BF16),
            pltpu.VMEM((8, 128, 768), BF16),
            pltpu.VMEM((8, 128, 768), BF16),
            pltpu.VMEM((8, 128, 768), BF16),
            pltpu.VMEM((8, 128, 768), BF16),
            pltpu.VMEM((128, 768), F32),
            pltpu.VMEM((2048, 768), F32),
            pltpu.VMEM((2048, 1), F32),
            pltpu.VMEM((8, 2, 48, 768), F32),
            pltpu.VMEM((8, 48, 768), BF16),
            pltpu.VMEM((8, 48, 768), BF16),
            pltpu.VMEM((8, 48, 768), BF16),
            pltpu.VMEM((8, 48, 768), BF16),
            pltpu.VMEM((48, 768), BF16),
            pltpu.VMEM((8, 48, 768), BF16),
            dma((4,)),
            dma((8,)),
            dma((9,)),
            dma((14,)),
            dma((14,)),
            dma((8,)),
            dma((8,)),
            dma((8,)),
            dma((8,)),
            dma((8,)),
            dma((8,)),
            dma((1,)),
            dma((1,)),
            dma((7,)),
            dma((8,)),
            dma((7,)),
            dma((8,)),
        ],
        compiler_params=pltpu.CompilerParams(
            collective_id=0, has_side_effects=True, vmem_limit_bytes=60 * 1024 * 1024
        ),
    )(images, head.T, tea_img, stu_txt, tea_txt)
    grad_images, grad_head, grad_text = pl.pallas_call(
        hand_over,
        name="hand_over",
        out_shape=tuple(jax.ShapeDtypeStruct(a.shape, a.dtype) for a in (grad_images, grad_head, grad_text)),
        in_specs=[vmem_spec] * 3,
        out_specs=(vmem_spec,) * 3,
    )(grad_images, grad_head, grad_text)
    return (grad_images, grad_head.T, grad_text)


def solution(mesh):
    placed = (
        P("dp", None),
        P(None, "tensor"),
        P("dp", None),
        P(("dp", "tensor"), None),
        P(("dp", "tensor"), None),
    )
    return jax.shard_map(
        per_device,
        mesh=mesh,
        in_specs=placed,
        out_specs=(P(("dp", "tensor"), None), P(None, "tensor"), P(("dp", "tensor"), None)),
        check_vma=False,
    )
```

```python
import functools

import jax
import jax.numpy as jnp
from jax import lax
from jax.experimental import pallas as pl
from jax.experimental.pallas import tpu as pltpu
from jax.sharding import PartitionSpec as P

logit_scale = 64.0
logit_bias = -2.0
loss_scale = 65536.0

F32 = jnp.float32
BF16 = jnp.bfloat16
MESH = pl.DeviceIdType.MESH
NT = (((1,), (1,)), ((), ()))
NN = (((1,), (0,)), ((), ()))
EPS = 1e-06


def dot(a, b, dims=NN):
    return lax.dot_general(a, b, dims, preferred_element_type=F32)


def unit_of(values):
    floats = values.astype(F32)
    length = jnp.sqrt(jnp.sum(floats * floats, axis=1, keepdims=True) + EPS)
    inverse = 1.0 / length
    return floats * inverse, inverse


def kernel(
    factor,
    images_hbm,
    head_ref,
    tea_hbm,
    txt_hbm,
    teatxt_hbm,
    gi_ref,
    gh_ref,
    gt_ref,
    images,
    tea,
    rawtxt,
    rawtea,
    headg,
    img,
    img_t,
    tbuf,
    gimg,
    gacc,
    gown,
    gstage,
    grecv,
    pstage,
    precv,
    rstage,
    rrecv,
    rown,
    units,
    invs,
    hacc,
    hpstage,
    hprecv,
    hrstage,
    hrrecv,
    xstage,
    xrecv,
    ystage,
    yrecv,
    lsem,
    hsend,
    hrecv,
    tsend,
    trecv,
    gsend,
    gsem,
    psend,
    psem,
    rsend,
    rsem,
    hpsend,
    hpsem,
    hrsend,
    hrsem,
    xsend,
    xsem,
    ysend,
    ysem,
):
    me_dp = lax.axis_index("dp")
    me_t = lax.axis_index("tensor")
    y_hi = me_dp // 4
    x = me_dp % 4
    chip = me_t // 2
    core = me_t % 2
    y_lo = me_t // 8
    z = chip % 4
    flip_t = (1 - y_lo) * 8 + me_t % 8
    mate = chip * 2 + (1 - core)

    def at_x(dx):
        return y_hi * 4 + lax.rem(x + dx, 4)

    def across_x(dx):
        return (1 - y_hi) * 4 + lax.rem(x + dx, 4)

    def group(dx, side):
        if side == 0:
            return (at_x(dx), me_t)
        return (across_x(dx), flip_t)

    def plane(j):
        return (me_dp, lax.rem(chip + j, 8) * 2 + core)

    def remote(src, dst, ssem, rsem_, device):
        return pltpu.make_async_remote_copy(
            src_ref=src, dst_ref=dst, send_sem=ssem, recv_sem=rsem_, device_id=device, device_id_type=MESH
        )

    loads = [
        pltpu.make_async_copy(txt_hbm, rawtxt, lsem.at[0]),
        pltpu.make_async_copy(teatxt_hbm, rawtea, lsem.at[1]),
        pltpu.make_async_copy(tea_hbm, tea, lsem.at[2]),
        pltpu.make_async_copy(images_hbm, images, lsem.at[3]),
    ]
    for load in loads:
        load.start()

    partners = [group(dx, side) for dx in range(4) for side in range(2) if (dx, side) != (0, 0)]
    partners += [plane(j) for j in range(1, 8)] + [(me_dp, mate)]
    partners += [((1 - y_hi) * 4 + x, me_t)]
    barrier = pltpu.get_barrier_semaphore()
    for device in partners:
        pl.semaphore_signal(barrier, inc=1, device_id=device, device_id_type=MESH)

    loads[0].wait()
    tbuf[0, 0:128, 0:768] = unit_of(rawtxt[...])[0].astype(BF16)
    loads[1].wait()
    tbuf[0, 0:128, 768:2304] = unit_of(rawtea[...])[0].astype(BF16)
    headg[chip, core] = head_ref[...]

    pl.semaphore_wait(barrier, len(partners))

    sends = []

    places = [
        (0, 128), (0, 192),
        (1, 0), (1, 64),
        (1, 128), (1, 192),
        (2, 0), (2, 64),
        (2, 128), (3, 64),
        (2, 192), (3, 0),
        (3, 128), (3, 192),
    ]

    def text_at(place):
        return tbuf.at[place[0], pl.ds(place[1], 64)]

    def send_text(src, index, send, device):
        copy = remote(text_at(src), text_at(places[index]), tsend.at[send], trecv.at[index], device)
        copy.start()
        sends.append(copy)

    def wait_text(*indices):
        for index in indices:
            ref = text_at(places[index])
            remote(ref, ref, tsend.at[0], trecv.at[index], across).wait_recv()

    across, ahead, behind = group(0, 1), group(1, 0), group(3, 0)
    own_low, own_high = (0, 0), (0, 64)
    send_text(own_low, 0, 0, across)
    send_text(own_low, 4, 1, ahead)
    send_text(own_high, 3, 2, behind)
    send_text(own_high, 1, 3, across)
    send_text(own_high, 5, 4, ahead)
    send_text(own_low, 2, 5, behind)

    heads = [
        remote(head_ref, headg.at[chip, core], hsend.at[j - 1], hrecv.at[chip], plane(j)) for j in range(1, 8)
    ]
    for copy in heads:
        copy.start()
    sends += heads

    loads[2].wait()

    @pl.loop(0, 32)
    def _(i):
        rows = pl.ds(pl.multiple_of(i * 64, 64), 64)
        tea[rows, :] = unit_of(tea[rows, :])[0].astype(BF16)

    for j in range(1, 8):
        other = lax.rem(chip + j, 8)
        remote(head_ref, headg.at[other, core], hsend.at[j - 1], hrecv.at[other], plane(j)).wait_recv()
    to_mate = remote(headg.at[:, core], headg.at[:, core], hsend.at[7], hrecv.at[8], (me_dp, mate))
    to_mate.start()
    sends.append(to_mate)
    loads[3].wait()
    remote(headg.at[:, 1 - core], headg.at[:, 1 - core], hsend.at[7], hrecv.at[8], (me_dp, mate)).wait_recv()

    def head_all():
        return headg[...].reshape(768, 768)

    def project(r):
        rows = pl.ds(pl.multiple_of(r * 256, 256), 256)
        proj = dot(images[rows, :], head_all(), NT).astype(BF16)
        unit, inverse = unit_of(proj)
        units[rows, :] = unit
        invs[rows, :] = inverse
        img[rows, :] = unit.astype(BF16)
        img_t[r] = unit.T.astype(BF16)

    @pl.loop(0, 4)
    def _(r):
        project(r)

    wait_text(4, 3)
    send_text(places[4], 6, 6, ahead)
    send_text(places[3], 7, 7, behind)
    wait_text(0)
    send_text(places[0], 8, 8, ahead)
    send_text(places[0], 10, 11, behind)

    @pl.loop(4, 8)
    def _(r):
        project(r)

    def coef_of(step, r):
        rows = pl.ds(pl.multiple_of(r * 256, 256), 256)
        target = dot(tea[rows, :], tbuf[step, :, 768:2304], NT)
        student = dot(img[rows, :], tbuf[step, :, 0:768], NT)
        half = 0.5 * logit_scale
        return (
            (jnp.tanh(half * student + 0.5 * logit_bias) - jnp.tanh(half * target + 0.5 * logit_bias))
            * (0.5 * factor)
        ).astype(BF16)

    def grads_of(step, r, coef, first):
        rows = pl.ds(pl.multiple_of(r * 256, 256), 256)
        part = dot(coef, tbuf[step, :, 0:768])
        if step == 0:
            gimg[rows, :] = part
        else:
            gimg[rows, :] += part
        text_part = dot(img_t[r], coef)
        if first:
            gacc[...] = text_part
        else:
            gacc[...] += text_part

    def run_step(step, pause=None, meanwhile=None):
        coef = coef_of(step, 0)
        for r in range(8):
            if r == pause:
                meanwhile()
            later = coef_of(step, r + 1) if r < 7 else None
            grads_of(step, r, coef, r == 0)
            coef = later

    owners = [None, across, ahead, behind, group(2, 0), group(3, 1), group(1, 1), group(2, 1)]
    mirror = [0, 1, 3, 2, 4, 6, 5, 7]

    def send_text_grad(block):
        copy = remote(
            gstage.at[block],
            grecv.at[mirror[block]],
            gsend.at[block],
            gsem.at[mirror[block]],
            owners[block],
        )
        copy.start()
        sends.append(copy)

    wait_text(1)
    send_text(places[1], 9, 10, ahead)
    send_text(places[1], 11, 9, behind)
    run_step(0)
    gown[...] = gacc[:, 0:128]
    gstage[1] = gacc[:, 128:256].astype(BF16)

    wait_text(2, 5)

    def second_across():
        wait_text(6, 7)
        send_text(places[6], 12, 12, across)
        send_text(places[7], 13, 13, across)
        send_text_grad(1)

    run_step(1, 5, second_across)
    gstage[2] = gacc[:, 0:128].astype(BF16)
    gstage[3] = gacc[:, 128:256].astype(BF16)

    wait_text(8, 10)
    run_step(2)
    gstage[4] = gacc[:, 0:128].astype(BF16)
    gstage[5, :, 0:64] = gacc[:, 128:192].astype(BF16)
    gstage[6, :, 0:64] = gacc[:, 192:256].astype(BF16)

    for block in (2, 3, 4):
        send_text_grad(block)
    wait_text(9, 11, 12, 13)

    route = [(1, 1), (0, 3), (1, 3), (0, 1), (1, 0), (1, 2), (0, 2), (0, 0)]

    def owner(k):
        dy, dz = route[k]
        return lax.rem(y_lo + dy, 2) * 4 + lax.rem(z + dz, 4)

    def from_mate(k):
        return remote(pstage.at[k], precv.at[k], psend.at[k], psem.at[k], (me_dp, mate))

    def to_owner(k):
        return remote(rstage.at[k], rrecv.at[chip], rsend.at[k], rsem.at[chip], (me_dp, owner(k) * 2 + core))

    def to_mate_part(k):
        theirs = pl.ds(pl.multiple_of(owner(k) * 256 + (1 - core) * 128, 128), 128)
        pstage[k] = gimg[theirs, :].astype(BF16)
        from_mate(k).start()

    def chip_sum(k):
        mine = pl.ds(pl.multiple_of(owner(k) * 256 + core * 128, 128), 128)
        from_mate(k).wait_recv()
        return gimg[mine, :] + precv[k].astype(F32)

    lag, early = 3, 3
    pieces = {}

    def take(k):
        mine = pl.ds(pl.multiple_of(owner(k) * 256 + core * 128, 128), 128)
        total = chip_sum(k)
        if k < 7:
            rstage[k] = total.astype(BF16)
        else:
            rown[...] = total
        if k < early:
            to_owner(k).start()
        unit = units[mine, :]
        row_dot = jnp.sum(unit * total, axis=1, keepdims=True)
        grad_proj = (total - unit * row_dot) * invs[mine, :]
        pieces[k] = (grad_proj.T.astype(BF16), images[mine, :])
        if k % 2:
            left = jnp.concatenate([pieces[k - 1][0], pieces[k][0]], axis=1)
            right = jnp.concatenate([pieces[k - 1][1], pieces[k][1]], axis=0)
            part = dot(left, right).reshape(8, 2, 48, 768)
            if k == 1:
                hacc[...] = part
            else:
                hacc[...] += part

    coef = coef_of(3, owner(0))
    for k in range(8):
        later = coef_of(3, owner(k + 1)) if k < 7 else None
        grads_of(3, owner(k), coef, k == 0)
        to_mate_part(k)
        if k >= lag:
            take(k - lag)
        coef = later
    for k in range(8 - lag, 8):
        take(k)

    hpstage[...] = hacc[:, 1 - core].astype(BF16)
    head_swap = remote(hpstage, hprecv, hpsend.at[0], hpsem.at[0], (me_dp, mate))
    head_swap.start()
    sends.append(head_swap)

    gstage[6, :, 64:128] = gacc[:, 0:64].astype(BF16)
    gstage[5, :, 64:128] = gacc[:, 64:128].astype(BF16)
    gstage[7] = gacc[:, 128:256].astype(BF16)
    for block in (5, 6, 7):
        send_text_grad(block)

    head_swap.wait_recv()
    hrstage[...] = (hacc[:, core] + hprecv[...].astype(F32)).astype(BF16)
    for j in range(1, 8):
        other = lax.rem(chip + j, 8)
        copy = remote(hrstage.at[other], hrrecv.at[chip], hrsend.at[j - 1], hrsem.at[chip], plane(j))
        copy.start()
        sends.append(copy)

    for k in range(early, 7):
        to_owner(k).start()

    head_sum = hrstage[chip].astype(F32)
    for j in range(1, 8):
        other = lax.rem(chip + j, 8)
        remote(hrstage.at[0], hrrecv.at[other], hrsend.at[0], hrsem.at[other], plane(j)).wait_recv()
        head_sum = head_sum + hrrecv[other].astype(F32)
    xstage[...] = head_sum.astype(BF16)
    xrecv[x] = xstage[...]
    for j in range(1, 4):
        copy = remote(xstage, xrecv.at[x], xsend.at[j - 1], xsem.at[x], (at_x(j), me_t))
        copy.start()
        sends.append(copy)

    text_sum = gown[...]
    for block in range(1, 8):
        remote(gstage.at[block], grecv.at[block], gsend.at[block], gsem.at[block], across).wait_recv()
        text_sum = text_sum + grecv[block].astype(F32)
    text_grad = text_sum.T
    unit, inverse = unit_of(rawtxt[...])
    gt_ref[...] = (text_grad - unit * jnp.sum(unit * text_grad, axis=1, keepdims=True)) * inverse

    for j in range(1, 4):
        other = lax.rem(x + j, 4)
        remote(xstage, xrecv.at[other], xsend.at[j - 1], xsem.at[other], (at_x(j), me_t)).wait_recv()
    ystage[...] = (
        (xrecv[0].astype(F32) + xrecv[1].astype(F32)) + (xrecv[2].astype(F32) + xrecv[3].astype(F32))
    ).astype(BF16)
    swap = remote(ystage, yrecv, ysend.at[0], ysem.at[0], ((1 - y_hi) * 4 + x, me_t))
    swap.start()
    sends.append(swap)

    for j in range(1, 8):
        other = lax.rem(chip + j, 8)
        remote(rstage.at[0], rrecv.at[other], rsend.at[0], rsem.at[other], plane(j)).wait_recv()
        rown[...] += rrecv[other].astype(F32)
    own_rows = pl.ds(pl.multiple_of(me_t * 128, 128), 128)
    total, unit = rown[...], units[own_rows, :]
    row_dot = jnp.sum(unit * total, axis=1, keepdims=True)
    grad_proj = (total - unit * row_dot) * invs[own_rows, :]
    gi_ref[...] = dot(grad_proj.astype(BF16), head_all())

    swap.wait_recv()
    gh_ref[...] = ystage[...].astype(F32) + yrecv[...].astype(F32)

    for copy in sends:
        copy.wait_send()

    for k in range(8):
        from_mate(k).wait_send()
        if k < 7:
            to_owner(k).wait_send()


def hand_over(*refs):
    half = len(refs) // 2
    for source, target in zip(refs[:half], refs[half:]):
        target[...] = source[...]


def per_device(images, head, tea_img, stu_txt, tea_txt):
    factor = logit_scale * loss_scale / (images.shape[0] * lax.axis_size("dp"))
    any_spec = pl.BlockSpec(memory_space=pl.ANY)
    vmem_spec = pl.BlockSpec(memory_space=pltpu.VMEM)
    dma = pltpu.SemaphoreType.DMA
    grad_images, grad_head, grad_text = pl.pallas_call(
        functools.partial(kernel, factor),
        name="distill",
        out_shape=(
            jax.ShapeDtypeStruct((128, 768), F32),
            jax.ShapeDtypeStruct((48, 768), F32),
            jax.ShapeDtypeStruct((128, 768), F32),
        ),
        in_specs=[any_spec, vmem_spec, any_spec, any_spec, any_spec],
        out_specs=(vmem_spec, vmem_spec, vmem_spec),
        scratch_shapes=[
            pltpu.VMEM((2048, 768), BF16),
            pltpu.VMEM((2048, 1536), BF16),
            pltpu.VMEM((128, 768), BF16),
            pltpu.VMEM((128, 1536), BF16),
            pltpu.VMEM((8, 2, 48, 768), BF16),
            pltpu.VMEM((2048, 768), BF16),
            pltpu.VMEM((8, 768, 256), BF16),
            pltpu.VMEM((4, 256, 2304), BF16),
            pltpu.VMEM((2048, 768), F32),
            pltpu.VMEM((768, 256), F32),
            pltpu.VMEM((768, 128), F32),
            pltpu.VMEM((8, 768, 128), BF16),
            pltpu.VMEM((8, 768, 128), BF16),
            pltpu.VMEM((8, 128, 768), BF16),
            pltpu.VMEM((8, 128, 768), BF16),
            pltpu.VMEM((8, 128, 768), BF16),
            pltpu.VMEM((8, 128, 768), BF16),
            pltpu.VMEM((128, 768), F32),
            pltpu.VMEM((2048, 768), F32),
            pltpu.VMEM((2048, 1), F32),
            pltpu.VMEM((8, 2, 48, 768), F32),
            pltpu.VMEM((8, 48, 768), BF16),
            pltpu.VMEM((8, 48, 768), BF16),
            pltpu.VMEM((8, 48, 768), BF16),
            pltpu.VMEM((8, 48, 768), BF16),
            pltpu.VMEM((48, 768), BF16),
            pltpu.VMEM((4, 48, 768), BF16),
            pltpu.VMEM((48, 768), BF16),
            pltpu.VMEM((48, 768), BF16),
            dma((4,)),
            dma((8,)),
            dma((9,)),
            dma((14,)),
            dma((14,)),
            dma((8,)),
            dma((8,)),
            dma((8,)),
            dma((8,)),
            dma((8,)),
            dma((8,)),
            dma((1,)),
            dma((1,)),
            dma((7,)),
            dma((8,)),
            dma((3,)),
            dma((4,)),
            dma((1,)),
            dma((1,)),
        ],
        compiler_params=pltpu.CompilerParams(
            collective_id=0, has_side_effects=True, vmem_limit_bytes=60 * 1024 * 1024
        ),
    )(images, head.T, tea_img, stu_txt, tea_txt)
    grad_images, grad_head, grad_text = pl.pallas_call(
        hand_over,
        name="hand_over",
        out_shape=tuple(jax.ShapeDtypeStruct(a.shape, a.dtype) for a in (grad_images, grad_head, grad_text)),
        in_specs=[vmem_spec] * 3,
        out_specs=(vmem_spec,) * 3,
    )(grad_images, grad_head, grad_text)
    return (grad_images, grad_head.T, grad_text)


def solution(mesh):
    placed = (
        P("dp", None),
        P(None, "tensor"),
        P("dp", None),
        P(("dp", "tensor"), None),
        P(("dp", "tensor"), None),
    )
    return jax.shard_map(
        per_device,
        mesh=mesh,
        in_specs=placed,
        out_specs=(P(("dp", "tensor"), None), P(None, "tensor"), P(("dp", "tensor"), None)),
        check_vma=False,
    )
```

```python
import functools

import jax
import jax.numpy as jnp
from jax import lax
from jax.experimental import pallas as pl
from jax.experimental.pallas import tpu as pltpu
from jax.sharding import PartitionSpec as P

logit_scale = 64.0
logit_bias = -2.0
loss_scale = 65536.0

F32 = jnp.float32
BF16 = jnp.bfloat16
MESH = pl.DeviceIdType.MESH
NT = (((1,), (1,)), ((), ()))
NN = (((1,), (0,)), ((), ()))
EPS = 1e-06


def dot(a, b, dims=NN):
    return lax.dot_general(a, b, dims, preferred_element_type=F32)


def unit_of(values):
    floats = values.astype(F32)
    length = jnp.sqrt(jnp.sum(floats * floats, axis=1, keepdims=True) + EPS)
    inverse = 1.0 / length
    return floats * inverse, inverse


def kernel(
    factor,
    images_hbm,
    head_ref,
    tea_hbm,
    txt_hbm,
    teatxt_hbm,
    gi_ref,
    gh_ref,
    gt_ref,
    images,
    tea,
    rawtxt,
    rawtea,
    headg,
    img,
    img_t,
    tbuf,
    gimg,
    gacc,
    gown,
    gstage,
    grecv,
    pstage,
    precv,
    rstage,
    rrecv,
    rown,
    units,
    invs,
    hacc,
    hpstage,
    hprecv,
    hrstage,
    hrrecv,
    xstage,
    xrecv,
    ystage,
    yrecv,
    lsem,
    hsend,
    hrecv,
    tsend,
    trecv,
    gsend,
    gsem,
    psend,
    psem,
    rsend,
    rsem,
    hpsend,
    hpsem,
    hrsend,
    hrsem,
    xsend,
    xsem,
    ysend,
    ysem,
):
    me_dp = lax.axis_index("dp")
    me_t = lax.axis_index("tensor")
    y_hi = me_dp // 4
    x = me_dp % 4
    chip = me_t // 2
    core = me_t % 2
    y_lo = me_t // 8
    z = chip % 4
    flip_t = (1 - y_lo) * 8 + me_t % 8
    mate = chip * 2 + (1 - core)

    def at_x(dx):
        return y_hi * 4 + lax.rem(x + dx, 4)

    def across_x(dx):
        return (1 - y_hi) * 4 + lax.rem(x + dx, 4)

    def group(dx, side):
        if side == 0:
            return (at_x(dx), me_t)
        return (across_x(dx), flip_t)

    def plane(j):
        return (me_dp, lax.rem(chip + j, 8) * 2 + core)

    def remote(src, dst, ssem, rsem_, device):
        return pltpu.make_async_remote_copy(
            src_ref=src, dst_ref=dst, send_sem=ssem, recv_sem=rsem_, device_id=device, device_id_type=MESH
        )

    loads = [
        pltpu.make_async_copy(txt_hbm, rawtxt, lsem.at[0]),
        pltpu.make_async_copy(teatxt_hbm, rawtea, lsem.at[1]),
        pltpu.make_async_copy(tea_hbm, tea, lsem.at[2]),
        pltpu.make_async_copy(images_hbm, images, lsem.at[3]),
    ]
    for load in loads:
        load.start()

    partners = [group(dx, side) for dx in range(4) for side in range(2) if (dx, side) != (0, 0)]
    partners += [plane(j) for j in range(1, 8)] + [(me_dp, mate)]
    partners += [((1 - y_hi) * 4 + x, me_t)]
    barrier = pltpu.get_barrier_semaphore()
    for device in partners:
        pl.semaphore_signal(barrier, inc=1, device_id=device, device_id_type=MESH)

    loads[0].wait()
    tbuf[0, 0:128, 0:768] = unit_of(rawtxt[...])[0].astype(BF16)
    loads[1].wait()
    tbuf[0, 0:128, 768:2304] = unit_of(rawtea[...])[0].astype(BF16)
    headg[chip, core] = head_ref[...]

    pl.semaphore_wait(barrier, len(partners))

    sends = []

    places = [
        (0, 128), (0, 192),
        (1, 0), (1, 64),
        (1, 128), (1, 192),
        (2, 0), (2, 64),
        (2, 128), (3, 64),
        (2, 192), (3, 0),
        (3, 128), (3, 192),
    ]

    def text_at(place):
        return tbuf.at[place[0], pl.ds(place[1], 64)]

    def send_text(src, index, send, device):
        copy = remote(text_at(src), text_at(places[index]), tsend.at[send], trecv.at[index], device)
        copy.start()
        sends.append(copy)

    def wait_text(*indices):
        for index in indices:
            ref = text_at(places[index])
            remote(ref, ref, tsend.at[0], trecv.at[index], across).wait_recv()

    across, ahead, behind = group(0, 1), group(1, 0), group(3, 0)
    own_low, own_high = (0, 0), (0, 64)
    send_text(own_low, 0, 0, across)
    send_text(own_low, 4, 1, ahead)
    send_text(own_high, 3, 2, behind)
    send_text(own_high, 1, 3, across)
    send_text(own_high, 5, 4, ahead)
    send_text(own_low, 2, 5, behind)

    heads = [
        remote(head_ref, headg.at[chip, core], hsend.at[j - 1], hrecv.at[chip], plane(j)) for j in range(1, 8)
    ]
    for copy in heads:
        copy.start()
    sends += heads

    loads[2].wait()

    @pl.loop(0, 32)
    def _(i):
        rows = pl.ds(pl.multiple_of(i * 64, 64), 64)
        tea[rows, :] = unit_of(tea[rows, :])[0].astype(BF16)

    for j in range(1, 8):
        other = lax.rem(chip + j, 8)
        remote(head_ref, headg.at[other, core], hsend.at[j - 1], hrecv.at[other], plane(j)).wait_recv()
    to_mate = remote(headg.at[:, core], headg.at[:, core], hsend.at[7], hrecv.at[8], (me_dp, mate))
    to_mate.start()
    sends.append(to_mate)
    loads[3].wait()
    remote(headg.at[:, 1 - core], headg.at[:, 1 - core], hsend.at[7], hrecv.at[8], (me_dp, mate)).wait_recv()

    def head_all():
        return headg[...].reshape(768, 768)

    def project(r):
        rows = pl.ds(pl.multiple_of(r * 256, 256), 256)
        proj = dot(images[rows, :], head_all(), NT).astype(BF16)
        unit, inverse = unit_of(proj)
        units[rows, :] = unit
        invs[rows, :] = inverse
        img[rows, :] = unit.astype(BF16)
        img_t[r] = unit.T.astype(BF16)

    @pl.loop(0, 4)
    def _(r):
        project(r)

    wait_text(4, 3)
    send_text(places[4], 6, 6, ahead)
    send_text(places[3], 7, 7, behind)
    wait_text(0)
    send_text(places[0], 8, 8, ahead)
    send_text(places[0], 10, 11, behind)

    @pl.loop(4, 8)
    def _(r):
        project(r)

    def coef_of(step, r):
        rows = pl.ds(pl.multiple_of(r * 256, 256), 256)
        target = dot(tea[rows, :], tbuf[step, :, 768:2304], NT)
        student = dot(img[rows, :], tbuf[step, :, 0:768], NT)
        half = 0.5 * logit_scale
        return (
            (jnp.tanh(half * student + 0.5 * logit_bias) - jnp.tanh(half * target + 0.5 * logit_bias))
            * (0.5 * factor)
        ).astype(BF16)

    def grads_of(step, r, coef, first):
        rows = pl.ds(pl.multiple_of(r * 256, 256), 256)
        part = dot(coef, tbuf[step, :, 0:768])
        if step == 0:
            gimg[rows, :] = part
        else:
            gimg[rows, :] += part
        text_part = dot(img_t[r], coef)
        if first:
            gacc[...] = text_part
        else:
            gacc[...] += text_part

    def run_step(step, pause=None, meanwhile=None):
        coef = coef_of(step, 0)
        for r in range(8):
            if r == pause:
                meanwhile()
            later = coef_of(step, r + 1) if r < 7 else None
            grads_of(step, r, coef, r == 0)
            coef = later

    owners = [None, across, ahead, behind, group(2, 0), group(3, 1), group(1, 1), group(2, 1)]
    mirror = [0, 1, 3, 2, 4, 6, 5, 7]

    def send_text_grad(block):
        copy = remote(
            gstage.at[block],
            grecv.at[mirror[block]],
            gsend.at[block],
            gsem.at[mirror[block]],
            owners[block],
        )
        copy.start()
        sends.append(copy)

    wait_text(1)
    send_text(places[1], 9, 10, ahead)
    send_text(places[1], 11, 9, behind)
    run_step(0)
    gown[...] = gacc[:, 0:128]
    gstage[1] = gacc[:, 128:256].astype(BF16)

    wait_text(2, 5)

    def second_across():
        wait_text(6, 7)
        send_text(places[6], 12, 12, across)
        send_text(places[7], 13, 13, across)
        send_text_grad(1)

    run_step(1, 2, second_across)
    gstage[2] = gacc[:, 0:128].astype(BF16)
    gstage[3] = gacc[:, 128:256].astype(BF16)

    wait_text(8, 10)
    run_step(2)
    gstage[4] = gacc[:, 0:128].astype(BF16)
    gstage[5, :, 0:64] = gacc[:, 128:192].astype(BF16)
    gstage[6, :, 0:64] = gacc[:, 192:256].astype(BF16)

    for block in (2, 3, 4):
        send_text_grad(block)
    wait_text(9, 11, 12, 13)

    route = [(1, 1), (0, 3), (1, 3), (0, 1), (1, 0), (1, 2), (0, 2), (0, 0)]

    def owner(k):
        dy, dz = route[k]
        return lax.rem(y_lo + dy, 2) * 4 + lax.rem(z + dz, 4)

    def from_mate(k):
        return remote(pstage.at[k], precv.at[k], psend.at[k], psem.at[k], (me_dp, mate))

    def to_owner(k):
        return remote(rstage.at[k], rrecv.at[chip], rsend.at[k], rsem.at[chip], (me_dp, owner(k) * 2 + core))

    def to_mate_part(k):
        theirs = pl.ds(pl.multiple_of(owner(k) * 256 + (1 - core) * 128, 128), 128)
        pstage[k] = gimg[theirs, :].astype(BF16)
        from_mate(k).start()

    def chip_sum(k):
        mine = pl.ds(pl.multiple_of(owner(k) * 256 + core * 128, 128), 128)
        from_mate(k).wait_recv()
        return gimg[mine, :] + precv[k].astype(F32)

    lag, early = 2, 3
    pieces = {}

    def take(k):
        mine = pl.ds(pl.multiple_of(owner(k) * 256 + core * 128, 128), 128)
        total = chip_sum(k)
        if k < 7:
            rstage[k] = total.astype(BF16)
        else:
            rown[...] = total
        if k < early:
            to_owner(k).start()
        unit = units[mine, :]
        row_dot = jnp.sum(unit * total, axis=1, keepdims=True)
        grad_proj = (total - unit * row_dot) * invs[mine, :]
        pieces[k] = (grad_proj.astype(BF16).T, images[mine, :])
        if k % 4 == 3:
            left = jnp.concatenate([pieces[n][0] for n in range(k - 3, k + 1)], axis=1)
            right = jnp.concatenate([pieces[n][1] for n in range(k - 3, k + 1)], axis=0)
            part = dot(left, right).reshape(8, 2, 48, 768)
            if k == 3:
                hacc[...] = part
            else:
                hacc[...] += part

    coef = coef_of(3, owner(0))
    for k in range(8):
        later = coef_of(3, owner(k + 1)) if k < 7 else None
        grads_of(3, owner(k), coef, k == 0)
        to_mate_part(k)
        if k >= lag:
            take(k - lag)
        coef = later
    for k in range(8 - lag, 8):
        take(k)

    hpstage[...] = hacc[:, 1 - core].astype(BF16)
    head_swap = remote(hpstage, hprecv, hpsend.at[0], hpsem.at[0], (me_dp, mate))
    head_swap.start()
    sends.append(head_swap)

    gstage[6, :, 64:128] = gacc[:, 0:64].astype(BF16)
    gstage[5, :, 64:128] = gacc[:, 64:128].astype(BF16)
    gstage[7] = gacc[:, 128:256].astype(BF16)
    for block in (5, 6, 7):
        send_text_grad(block)

    head_swap.wait_recv()
    hrstage[...] = (hacc[:, core] + hprecv[...].astype(F32)).astype(BF16)
    for j in range(1, 8):
        other = lax.rem(chip + j, 8)
        copy = remote(hrstage.at[other], hrrecv.at[chip], hrsend.at[j - 1], hrsem.at[chip], plane(j))
        copy.start()
        sends.append(copy)

    for k in range(early, 7):
        to_owner(k).start()

    head_sum = hrstage[chip].astype(F32)
    for j in range(1, 8):
        other = lax.rem(chip + j, 8)
        remote(hrstage.at[0], hrrecv.at[other], hrsend.at[0], hrsem.at[other], plane(j)).wait_recv()
        head_sum = head_sum + hrrecv[other].astype(F32)
    xstage[...] = head_sum.astype(BF16)
    xrecv[x] = xstage[...]
    for j in range(1, 4):
        copy = remote(xstage, xrecv.at[x], xsend.at[j - 1], xsem.at[x], (at_x(j), me_t))
        copy.start()
        sends.append(copy)

    text_sum = gown[...]
    for block in range(1, 8):
        remote(gstage.at[block], grecv.at[block], gsend.at[block], gsem.at[block], across).wait_recv()
        text_sum = text_sum + grecv[block].astype(F32)
    text_grad = text_sum.T
    unit, inverse = unit_of(rawtxt[...])
    gt_ref[...] = (text_grad - unit * jnp.sum(unit * text_grad, axis=1, keepdims=True)) * inverse

    for j in range(1, 4):
        other = lax.rem(x + j, 4)
        remote(xstage, xrecv.at[other], xsend.at[j - 1], xsem.at[other], (at_x(j), me_t)).wait_recv()
    ystage[...] = (
        (xrecv[0].astype(F32) + xrecv[1].astype(F32)) + (xrecv[2].astype(F32) + xrecv[3].astype(F32))
    ).astype(BF16)
    swap = remote(ystage, yrecv, ysend.at[0], ysem.at[0], ((1 - y_hi) * 4 + x, me_t))
    swap.start()
    sends.append(swap)

    for j in range(1, 8):
        other = lax.rem(chip + j, 8)
        remote(rstage.at[0], rrecv.at[other], rsend.at[0], rsem.at[other], plane(j)).wait_recv()
        rown[...] += rrecv[other].astype(F32)
    own_rows = pl.ds(pl.multiple_of(me_t * 128, 128), 128)
    total, unit = rown[...], units[own_rows, :]
    row_dot = jnp.sum(unit * total, axis=1, keepdims=True)
    grad_proj = (total - unit * row_dot) * invs[own_rows, :]
    gi_ref[...] = dot(grad_proj.astype(BF16), head_all())

    swap.wait_recv()
    gh_ref[...] = ystage[...].astype(F32) + yrecv[...].astype(F32)

    for copy in sends:
        copy.wait_send()

    for k in range(8):
        from_mate(k).wait_send()
        if k < 7:
            to_owner(k).wait_send()


def hand_over(*refs):
    half = len(refs) // 2
    for source, target in zip(refs[:half], refs[half:]):
        target[...] = source[...]


def per_device(images, head, tea_img, stu_txt, tea_txt):
    factor = logit_scale * loss_scale / (images.shape[0] * lax.axis_size("dp"))
    any_spec = pl.BlockSpec(memory_space=pl.ANY)
    vmem_spec = pl.BlockSpec(memory_space=pltpu.VMEM)
    dma = pltpu.SemaphoreType.DMA
    grad_images, grad_head, grad_text = pl.pallas_call(
        functools.partial(kernel, factor),
        name="distill",
        out_shape=(
            jax.ShapeDtypeStruct((128, 768), F32),
            jax.ShapeDtypeStruct((48, 768), F32),
            jax.ShapeDtypeStruct((128, 768), F32),
        ),
        in_specs=[any_spec, vmem_spec, any_spec, any_spec, any_spec],
        out_specs=(vmem_spec, vmem_spec, vmem_spec),
        scratch_shapes=[
            pltpu.VMEM((2048, 768), BF16),
            pltpu.VMEM((2048, 1536), BF16),
            pltpu.VMEM((128, 768), BF16),
            pltpu.VMEM((128, 1536), BF16),
            pltpu.VMEM((8, 2, 48, 768), BF16),
            pltpu.VMEM((2048, 768), BF16),
            pltpu.VMEM((8, 768, 256), BF16),
            pltpu.VMEM((4, 256, 2304), BF16),
            pltpu.VMEM((2048, 768), F32),
            pltpu.VMEM((768, 256), F32),
            pltpu.VMEM((768, 128), F32),
            pltpu.VMEM((8, 768, 128), BF16),
            pltpu.VMEM((8, 768, 128), BF16),
            pltpu.VMEM((8, 128, 768), BF16),
            pltpu.VMEM((8, 128, 768), BF16),
            pltpu.VMEM((8, 128, 768), BF16),
            pltpu.VMEM((8, 128, 768), BF16),
            pltpu.VMEM((128, 768), F32),
            pltpu.VMEM((2048, 768), F32),
            pltpu.VMEM((2048, 1), F32),
            pltpu.VMEM((8, 2, 48, 768), F32),
            pltpu.VMEM((8, 48, 768), BF16),
            pltpu.VMEM((8, 48, 768), BF16),
            pltpu.VMEM((8, 48, 768), BF16),
            pltpu.VMEM((8, 48, 768), BF16),
            pltpu.VMEM((48, 768), BF16),
            pltpu.VMEM((4, 48, 768), BF16),
            pltpu.VMEM((48, 768), BF16),
            pltpu.VMEM((48, 768), BF16),
            dma((4,)),
            dma((8,)),
            dma((9,)),
            dma((14,)),
            dma((14,)),
            dma((8,)),
            dma((8,)),
            dma((8,)),
            dma((8,)),
            dma((8,)),
            dma((8,)),
            dma((1,)),
            dma((1,)),
            dma((7,)),
            dma((8,)),
            dma((3,)),
            dma((4,)),
            dma((1,)),
            dma((1,)),
        ],
        compiler_params=pltpu.CompilerParams(
            collective_id=0, has_side_effects=True, vmem_limit_bytes=60 * 1024 * 1024
        ),
    )(images, head.T, tea_img, stu_txt, tea_txt)
    grad_images, grad_head, grad_text = pl.pallas_call(
        hand_over,
        name="hand_over",
        out_shape=tuple(jax.ShapeDtypeStruct(a.shape, a.dtype) for a in (grad_images, grad_head, grad_text)),
        in_specs=[vmem_spec] * 3,
        out_specs=(vmem_spec,) * 3,
    )(grad_images, grad_head, grad_text)
    return (grad_images, grad_head.T, grad_text)


def solution(mesh):
    placed = (
        P("dp", None),
        P(None, "tensor"),
        P("dp", None),
        P(("dp", "tensor"), None),
        P(("dp", "tensor"), None),
    )
    return jax.shard_map(
        per_device,
        mesh=mesh,
        in_specs=placed,
        out_specs=(P(("dp", "tensor"), None), P(None, "tensor"), P(("dp", "tensor"), None)),
        check_vma=False,
    )
```
